32 devices in a mesh: gx: 4 (over z), gy: 4 (over y, x), gz: 2 (over core).
Axes of the slice: x: 2, y: 2, z: 4, core: 2. Of those that a mesh axis runs over, the one named last changes fastest.
Arguments:
- offsets: float32 [3, 131072], P(None, ('gx', 'gy', 'gz')), may hold values from 0 to 1
- strength: float32 [3, 131072], P(None, ('gx', 'gy', 'gz')), may hold values from -0.012 to 0.012
- ghost_list: int32 [49152], P(('gx', 'gy', 'gz')), may hold values from 0 to 4095
- pair_targets: int32 [4096], P(('gx', 'gy', 'gz')), may hold values from 0 to 31
- pair_sources: int32 [4096], P(('gx', 'gy', 'gz')), may hold values from 0 to 103
- owners: int32 [1024, 1], P(('gx', 'gy', 'gz')), may hold values from 0 to 15; in each aligned block of 32 rows (0 to 31, 32 to 63, ...) at most 4 rows name the same one
Outputs:
- moved_positions: float32 [2048, 3, 128], P(('gx', 'gy', 'gz'))
- moved_velocity: float32 [2048, 3, 128], P(('gx', 'gy', 'gz'))
The draws below stay inside these ranges and needn't reach their ends.
Inputs may be any that keep to these rules, and one draw needn't show every extreme that they name: `owners`: among the 32 blocks of one domain no owner is named more than 4 times.
All inputs are finite; a program needn't handle non-finite values.
Results may differ from the reference program's by a relative error of at most 0.0003.
Values sent between devices are 32-bit elements; how exact they have to be, the bound alone decides.
No kernel may reach another device: no remote copies, remote signals or barrier semaphores. Data moves between devices by JAX's collectives and lax.ppermute only.
A program may use at most 128 MiB of HBM per device.

```python
import math
import jax
import jax.numpy as jnp
import numpy as np
from jax import lax

SEG = 4096
ORDER = 5
GHOST = 1536
NPAIR = 128
CAP = 4
NSEG = 131072
N_GX = 4
N_GY = 4
N_GZ = 2
DEVICES = 32


def touch_ends(result, rng, low, high):
    spot = [jax.random.randint(jax.random.fold_in(rng, axis), (), 0, length) for axis, length in enumerate(result.shape)]
    widest = result.shape.index(max(result.shape))
    next_to = spot[:widest] + [(spot[widest] + 1) % result.shape[widest]] + spot[widest + 1:]
    return result.at[tuple(spot)].set(low).at[tuple(next_to)].set(high)


def steps_of(stream_key, extent, split, low, largest):
    loudness, own = 1.0, jax.random.fold_in(stream_key, 6)
    for axis_at, parts in split:
        steps = jnp.exp(jax.random.uniform(jax.random.fold_in(own, axis_at), (parts,), jnp.float32, low / len(split), largest / len(split)))
        loudness = loudness * jnp.repeat(steps, extent[axis_at] // parts).reshape([-1 if axis == axis_at else 1 for axis in range(len(extent))])
    return loudness


def shared_out(stream_key, own, number, rows, amount, top, reach, lean):
    ranking = jax.random.permutation(stream_key, amount)
    crowded, common = shares(amount, rows * top, reach, lean, True), shares(amount, rows * top, reach, lean, False)
    places = jnp.arange(amount)

    def named(tallies, offset_by):
        used = int((tallies > 0).sum())
        fixed = max(1, used // 4)
        moved = fixed + (places - fixed + offset_by * (used - fixed)) % max(1, amount - fixed)
        return jnp.zeros((amount,), jnp.int32).at[ranking[jnp.where(places < fixed, places, moved)]].set(jnp.asarray(tallies, jnp.int32))

    tallies = jnp.where(number % 4 == 0, named(crowded, number // 4), named(common, number - number // 4 - 1))
    mixed = jax.random.permutation(jax.random.fold_in(own, 3), amount)
    donor, receiver = mixed[0:amount // 2 * 2:2], mixed[1:amount // 2 * 2:2]
    slack = jnp.minimum(tallies[donor] - 1, reach - tallies[receiver]) // 2
    slack = jnp.where((donor == ranking[0]) | (receiver == ranking[0]) | (tallies[receiver] == 0), 0, jnp.maximum(slack, 0))
    moved = jax.random.randint(jax.random.fold_in(own, 4), (amount // 2,), 0, 1 << 20) % (slack + 1)
    tallies = tallies.at[donor].add(-moved).at[receiver].add(moved)
    labels = jnp.searchsorted(jnp.cumsum(tallies), jnp.arange(rows * top), side="right").astype(jnp.int32)
    grid = labels.reshape(top, rows).T
    grid = grid[jax.random.permutation(jax.random.fold_in(own, 1), rows)]
    offset_by = jax.random.randint(jax.random.fold_in(own, 2), (rows, 1), 0, top)
    return jnp.take_along_axis(grid, (jnp.arange(top)[None, :] + offset_by) % top, axis=1)


def shares(number_of, total, most, slope, full):
    portions = [(1 << 20) // math.isqrt(standing ** slope) + 1 for standing in range(1, number_of + 1)]
    largest = most if full else min(most, max(-(-total // number_of), total * portions[0] // sum(portions)))
    least = 1 if total - largest >= number_of - 1 else 0
    holding, rest = [largest] + [least] * (number_of - 1), total - largest - least * (number_of - 1)
    while rest > 0:
        free = [i for i in range(1, number_of) if holding[i] < largest] or [i for i in range(1, number_of) if holding[i] < most]
        mass, budget = sum([portions[i] for i in free]), rest
        for i in free:
            more = min(most - holding[i], max(1, budget * portions[i] // mass), rest)
            holding[i] = holding[i] + more
            rest = rest - more
    return np.array(holding)


def gaussian(key, shape, width, limit, cuts=(), kind=jnp.bfloat16):
    loudness = steps_of(key, shape, cuts, -0.22, 0.18) if cuts else 1.0
    values = jax.random.normal(key, shape, jnp.float32) * width * loudness
    return jnp.minimum(jnp.maximum(values, -limit), limit).astype(kind)


def setup_inputs(seed: int = 0) -> dict:
    arg_keys = jax.random.split(jax.random.key(seed), 7)
    offsets = jnp.clip(1.0 * jax.random.uniform(arg_keys[0], (3, NSEG), jnp.float32) ** steps_of(arg_keys[0], (3, NSEG), ((1, 32),), -0.2, 0.2), 0.0, 1.0)
    strength = gaussian(arg_keys[1], (3, NSEG), 0.002, 0.012, ((1, 32),), jnp.float32)
    ghost_list = touch_ends(jax.random.randint(arg_keys[2], (DEVICES * GHOST,), 0, SEG), jax.random.fold_in(arg_keys[2], 1), 0, SEG - 1).astype(jnp.int32)
    pair_targets = touch_ends(jax.random.randint(arg_keys[3], (DEVICES * NPAIR,), 0, SEG // 128), jax.random.fold_in(arg_keys[3], 1), 0, (SEG // 128) - 1).astype(jnp.int32)
    pair_sources = touch_ends(jax.random.randint(arg_keys[4], (DEVICES * NPAIR,), 0, SEG // 128 + 6 * (GHOST // 128)), jax.random.fold_in(arg_keys[4], 1), 0, (SEG // 128 + 6 * (GHOST // 128)) - 1).astype(jnp.int32)
    owners_keys = jax.random.split(jax.random.fold_in(arg_keys[5], 1), (DEVICES * SEG // 128) // (SEG // 128))
    owners_turns = jax.random.permutation(jax.random.fold_in(arg_keys[5], 3), (DEVICES * SEG // 128) // (SEG // 128))
    owners = jax.vmap(lambda own, number: shared_out(jax.random.fold_in(arg_keys[5], 2), own, number, SEG // 128, N_GX * N_GY, 1, CAP, 2))(owners_keys, owners_turns).reshape((DEVICES * SEG // 128, 1))
    return {"offsets": offsets, "strength": strength, "ghost_list": ghost_list, "pair_targets": pair_targets, "pair_sources": pair_sources, "owners": owners}


core_sq = 0.0025
time_step = 0.1
highest = lax.Precision.HIGHEST

def exponent_table():
    entries = []
    for degree in range(ORDER + 1):
        for leading in range(degree, -1, -1):
            for middle in range(degree - leading, -1, -1):
                entries.append((leading, middle, degree - leading - middle))
    return np.array(entries, dtype=np.int32)

def factorial_table():
    return np.array([float(np.prod([math.factorial(int(exponent)) for exponent in triple])) for triple in exponent_table()], dtype=np.float32)

def monomials(relative):
    powers = exponent_table()
    stacks = [jnp.stack([relative[axis_id] ** degree for degree in range(ORDER + 1)]) for axis_id in range(3)]
    return stacks[0][powers[:, 0]] * stacks[1][powers[:, 1]] * stacks[2][powers[:, 2]]

def derivative_tables():
    powers = exponent_table()
    factors = factorial_table()
    starts = np.cumsum([0] + [3 ** degree for degree in range(ORDER + 1)])
    entry_count = powers.shape[0]
    index_table = np.zeros((entry_count, entry_count), dtype=np.int32)
    weight_table = np.zeros((entry_count, entry_count), dtype=np.float32)
    for outer_pos in range(entry_count):
        for inner_pos in range(entry_count):
            merged = powers[outer_pos] + powers[inner_pos]
            degree = int(np.sum(merged))
            if degree <= ORDER:
                flat_pos = 0
                for axis_id in range(3):
                    for repeat in range(int(merged[axis_id])):
                        flat_pos = flat_pos * 3 + axis_id
                index_table[outer_pos, inner_pos] = starts[degree] + flat_pos
                weight_table[outer_pos, inner_pos] = (-1.0) ** int(np.sum(powers[inner_pos])) / float(factors[inner_pos])
    return (index_table, weight_table)

def potential(separation):
    return lax.rsqrt(jnp.sum(separation * separation) + core_sq)

def jacobian_of(function):

    def derived(separation):
        value, pullback = jax.vjp(function, separation)
        count = value.size
        basis = jnp.eye(count, dtype=value.dtype).reshape((count,) + value.shape)
        rows = jax.vmap(pullback)(basis)[0]
        return rows.reshape(value.shape + separation.shape)
    return derived

def kernel_derivatives(separation):
    pieces = []
    current = potential
    for degree in range(ORDER + 1):
        pieces.append(jnp.ravel(current(separation)))
        current = jacobian_of(current)
    return jnp.concatenate(pieces)

def local_expansion(separations, moments, weights):
    index_table, weight_table = derivative_tables()
    derivs = jax.vmap(kernel_derivatives)(separations)
    operator = derivs[:, index_table] * jnp.asarray(weight_table, jnp.float32)[None] * weights[:, None, None]
    return jnp.einsum('sba,sac->bc', operator, moments, precision=highest)

def far_field(relative, expansion):
    scaled = monomials(relative) / jnp.asarray(factorial_table(), jnp.float32)[:, None]
    return jnp.dot(expansion.T, scaled, precision=highest)

def moments_about(positions, strength, centre):
    return jnp.dot(monomials(positions - centre[:, None]), strength.T, precision=highest)

def far_sources(slab_centre, index_x, index_y, tall, column_moments):
    column_ids = jnp.arange(column_moments.shape[0], dtype=jnp.int32)
    column_x = column_ids // tall
    column_y = column_ids % tall
    column_centres = jnp.stack([column_x.astype(jnp.float32) + 0.5, column_y.astype(jnp.float32) + 0.5, jnp.full(column_ids.shape, 0.5, jnp.float32)], axis=1)
    column_weights = (jnp.maximum(jnp.abs(column_x - index_x), jnp.abs(column_y - index_y)) >= 3).astype(jnp.float32)
    separations = slab_centre[None, :] - column_centres
    return local_expansion(separations, column_moments, column_weights)

def near_field(positions, strength, ghosts, targets, sources):
    tile_count = positions.shape[1] // 128
    ghost_tiles = ghosts.shape[2] // 128
    own_pos = positions.reshape(3, tile_count, 128).transpose(1, 0, 2)
    own_str = strength.reshape(3, tile_count, 128).transpose(1, 0, 2)
    ghost_pos = ghosts[:, :3].reshape(6, 3, ghost_tiles, 128).transpose(0, 2, 1, 3).reshape(6 * ghost_tiles, 3, 128)
    ghost_str = ghosts[:, 3:].reshape(6, 3, ghost_tiles, 128).transpose(0, 2, 1, 3).reshape(6 * ghost_tiles, 3, 128)
    source_pos = jnp.concatenate([own_pos, ghost_pos])
    source_str = jnp.concatenate([own_str, ghost_str])
    pair_count = targets.shape[0]
    block_size = 64 if pair_count % 64 == 0 else pair_count
    target_blocks = targets.reshape(pair_count // block_size, block_size)
    source_blocks = sources.reshape(pair_count // block_size, block_size)
    tile_ids = jnp.arange(tile_count, dtype=jnp.int32)

    def accumulate(totals, pair_block):
        target_ids, source_ids = pair_block
        here = own_pos[target_ids]
        there = source_pos[source_ids]
        pushed = source_str[source_ids]
        gap = here[:, 0, :, None] - there[:, 0, None, :]
        dist_sq = gap * gap
        for axis_id in range(1, 3):
            gap = here[:, axis_id, :, None] - there[:, axis_id, None, :]
            dist_sq = dist_sq + gap * gap
        kernel_block = lax.rsqrt(dist_sq + core_sq)
        contrib = jnp.einsum('bij,bkj->bki', kernel_block, pushed, precision=highest)
        selector = (tile_ids[:, None] == target_ids[None, :]).astype(jnp.float32)
        return (totals + jnp.einsum('tb,bki->tki', selector, contrib, precision=highest), None)
    totals, unused = lax.scan(accumulate, jnp.zeros((tile_count, 3, 128), jnp.float32), (target_blocks, source_blocks))
    return totals.transpose(1, 0, 2).reshape(3, tile_count * 128)

def place_blocks(fields, owner_ids, group, capacity):
    block_count = owner_ids.shape[0]
    block_ids = jnp.arange(block_count, dtype=jnp.int32)
    earlier = (owner_ids[None, :] == owner_ids[:, None]) & (block_ids[None, :] < block_ids[:, None])
    slot_ids = owner_ids * capacity + lax.optimization_barrier(jnp.sum(earlier.astype(jnp.int32), axis=1))
    placer = (slot_ids[:, None] == jnp.arange(group * capacity, dtype=jnp.int32)[None, :]).astype(jnp.float32)
    tiles = fields.reshape(6, block_count, 128).transpose(1, 0, 2).reshape(block_count, 768)
    return jnp.dot(placer.T, tiles, precision=highest).reshape(group, capacity, 6, 128)

def from_lower(field, axis_id):
    length = field.shape[axis_id]
    kept = lax.slice_in_dim(field, 0, length - 1, axis=axis_id)
    return jnp.concatenate([jnp.zeros_like(lax.slice_in_dim(field, 0, 1, axis=axis_id)), kept], axis=axis_id)

def from_upper(field, axis_id):
    length = field.shape[axis_id]
    kept = lax.slice_in_dim(field, 1, length, axis=axis_id)
    return jnp.concatenate([kept, jnp.zeros_like(lax.slice_in_dim(field, 0, 1, axis=axis_id))], axis=axis_id)

def reference(offsets, strength, ghost_list, pair_targets, pair_sources, owners):
    group = N_GX * N_GY
    device_ids = jnp.arange(DEVICES, dtype=jnp.int32)
    index_x = device_ids // (N_GY * N_GZ)
    index_y = device_ids // N_GZ % N_GY
    index_z = device_ids % N_GZ
    side_z = 1.0 / N_GZ
    corners = jnp.stack([index_x.astype(jnp.float32), index_y.astype(jnp.float32), index_z.astype(jnp.float32) * side_z], axis=1)
    sides = jnp.asarray([1.0, 1.0, side_z], jnp.float32)
    positions = corners[:, :, None] + offsets.reshape(3, DEVICES, SEG).transpose(1, 0, 2) * sides[None, :, None]
    strength_dev = strength.reshape(3, DEVICES, SEG).transpose(1, 0, 2)
    slab_centres = corners + 0.5 * sides[None, :]
    column_centres = jnp.stack([index_x.astype(jnp.float32) + 0.5, index_y.astype(jnp.float32) + 0.5, jnp.full((DEVICES,), 0.5, jnp.float32)], axis=1)
    ghost_ids = ghost_list.reshape(DEVICES, GHOST)
    target_ids = pair_targets.reshape(DEVICES, NPAIR)
    source_ids = pair_sources.reshape(DEVICES, NPAIR)

    def leaf_moments(items):
        return moments_about(items[0], items[1], items[2])
    velocity = jnp.zeros_like(positions)
    for step_number in range(2):
        column_parts = lax.map(leaf_moments, (positions, strength_dev, column_centres))
        column_moments = lax.optimization_barrier(jnp.sum(column_parts.reshape(group, N_GZ, -1, 3), axis=1))
        packed = jnp.concatenate([positions, strength_dev], axis=1)
        chosen = jnp.take_along_axis(packed, ghost_ids[:, None, :], axis=2).reshape(N_GX, N_GY, N_GZ, 6, GHOST)
        neighbours = jnp.stack([from_lower(chosen, 0), from_upper(chosen, 0), from_lower(chosen, 1), from_upper(chosen, 1), from_lower(chosen, 2), from_upper(chosen, 2)], axis=3).reshape(DEVICES, 6, 6, GHOST)

        def device_forces(items):
            pos_here, str_here, ghost_here, target_here, source_here, device_id = items
            slab_centre = slab_centres[device_id]
            expansion = far_sources(slab_centre, index_x[device_id], index_y[device_id], N_GY, column_moments)
            near = near_field(pos_here, str_here, ghost_here, target_here, source_here)
            return near + far_field(pos_here - slab_centre[:, None], expansion)
        velocity = lax.map(device_forces, (positions, strength_dev, neighbours, target_ids, source_ids, device_ids))
        positions = positions + time_step * velocity
    data = jnp.concatenate([positions, velocity], axis=1)
    owner_rows = owners[:, 0].reshape(DEVICES, SEG // 128)

    def place_one(items):
        return place_blocks(items[0], items[1], group, CAP)
    sent = lax.map(place_one, (data, owner_rows))
    received = sent.reshape(N_GX, N_GY, N_GZ, N_GX, N_GY, CAP, 6, 128).transpose(3, 4, 2, 0, 1, 5, 6, 7).reshape(DEVICES * group * CAP, 6, 128)
    return (received[:, :3], received[:, 3:])
```

```python
import functools
import math

import jax
import jax.numpy as jnp
import numpy as np
from jax import lax
from jax.experimental import pallas as pl
from jax.experimental.pallas import tpu as pltpu
from jax.sharding import PartitionSpec as P

ORDER = 5
LANES = 128
ROWS = 8
FEATURES = 32
BATCH = 16

core_sq = 0.0025
time_step = 0.1
everywhere = ("gx", "gy", "gz")
f32 = jnp.float32
bf16 = jnp.bfloat16


def exponents():
    entries = []
    for degree in range(ORDER + 1):
        for leading in range(degree, -1, -1):
            for middle in range(degree - leading, -1, -1):
                entries.append((leading, middle, degree - leading - middle))
    return entries


POWERS = exponents()
TERMS = len(POWERS)
PLACE = {triple: spot for spot, triple in enumerate(POWERS)}
FACTORIAL = [float(np.prod([math.factorial(e) for e in triple])) for triple in POWERS]


def row_ids():
    return lax.broadcasted_iota(jnp.int32, (ROWS, LANES), 0)


def spread(ref, row):
    return ref[pl.ds(row, ROWS, stride=0), :]


def tile_of(ref, tile):
    return ref[pl.ds(pl.multiple_of(tile * ROWS, ROWS), ROWS), :]


def slab_middle(deep):
    side_z = 1.0 / deep
    middle_x = lax.axis_index("gx").astype(f32) + 0.5
    middle_y = lax.axis_index("gy").astype(f32) + 0.5
    middle_z = lax.axis_index("gz").astype(f32) * side_z + 0.5 * side_z
    return middle_x, middle_y, middle_z


def relative_pair(pack, pair, middle):
    low = row_ids() < 4
    base = pair * (2 * ROWS)
    return [
        jnp.where(low, spread(pack, base + axis), spread(pack, base + ROWS + axis)) - middle[axis]
        for axis in range(3)
    ]


def leaf_moments(pack, tiles, devices, leaf, work, line):
    middle_x, middle_y, _ = slab_middle(1)
    middle = (middle_x, middle_y, 0.5)
    low = row_ids() < 4

    def accumulate(chosen):
        def body(pair, sums):
            x, y, z = relative_pair(pack, pair, middle)
            even, odd = tile_of(pack, 2 * pair), tile_of(pack, 2 * pair + 1)
            first = jnp.where(low, pltpu.roll(even, 4, 0), odd)
            value = {(0, 0, 0): first}
            gained = []
            for a in range(ORDER + 1):
                if a > 0:
                    value[a, 0, 0] = value[a - 1, 0, 0] * x
                if a not in chosen:
                    continue
                for b in range(ORDER + 1 - a):
                    if b > 0:
                        value[a, b, 0] = value[a, b - 1, 0] * y
                    for c in range(ORDER + 1 - a - b):
                        if c > 0:
                            value[a, b, c] = value[a, b, c - 1] * z
                        gained.append(value[a, b, c])
            return tuple(total + more for total, more in zip(sums, gained))

        names = [
            (a, b, c)
            for a in chosen
            for b in range(ORDER + 1 - a)
            for c in range(ORDER + 1 - a - b)
        ]
        zero = jnp.zeros((ROWS, LANES), f32)
        sums = lax.fori_loop(0, tiles // 2, body, tuple(zero for _ in names))
        for name, total in zip(names, sums):
            spot = PLACE[name]
            factor = (-1.0) ** sum(name) / FACTORIAL[spot]
            work[spot * ROWS : (spot + 1) * ROWS, :] = total * factor

    accumulate((0,))
    accumulate((1, 2, 3, 4, 5))
    line[...] = jnp.zeros_like(line)
    for k in range(3):
        both = work[pl.ds(k, TERMS, stride=ROWS), :] + work[pl.ds(k + 4, TERMS, stride=ROWS), :]
        summed = jnp.sum(both.T, axis=0, keepdims=True)
        line[k : k + 1, 0:TERMS] = summed
        line[k + 4 : k + 5, 0:TERMS] = summed
    copies = line[...]
    for at in range(devices * 4 // ROWS):
        leaf[at * ROWS : (at + 1) * ROWS, :] = copies


def pick_ghosts(pack, tiles, ghost_ids, ghosts):
    for out_tile in range(ghost_ids.shape[0]):
        wanted = jnp.broadcast_to(ghost_ids[out_tile : out_tile + 1, :], (ROWS, LANES))
        lane, owner = wanted & (LANES - 1), wanted >> 7
        found = jnp.zeros((ROWS, LANES), f32)
        for tile in range(tiles):
            moved = jnp.take_along_axis(
                pack[tile * ROWS : (tile + 1) * ROWS, :], lane, axis=1, mode="promise_in_bounds"
            )
            found = jnp.where(owner == tile, moved, found)
        ghosts[out_tile * ROWS : (out_tile + 1) * ROWS, :] = found


def prologue_kernel(tiles, devices, deep, offsets, strength, ghost_ids, pack, leaf, ghosts, work, line):
    side_z = 1.0 / deep
    axis = lax.broadcasted_iota(jnp.int32, (3, LANES), 0)
    corner = jnp.where(
        axis == 0,
        lax.axis_index("gx").astype(f32),
        jnp.where(
            axis == 1, lax.axis_index("gy").astype(f32), lax.axis_index("gz").astype(f32) * side_z
        ),
    )
    sides = jnp.where(axis == 2, side_z, 1.0)
    blank = jnp.zeros((1, LANES), f32)
    for tile in range(tiles):
        span = slice(tile * LANES, (tile + 1) * LANES)
        base = tile * ROWS
        pack[base : base + 3, :] = corner + offsets[:, span] * sides
        pack[base + 3 : base + 4, :] = blank
        pack[base + 4 : base + 7, :] = strength[:, span]
        pack[base + 7 : base + 8, :] = blank
    leaf_moments(pack, tiles, devices, leaf, work, line)
    pick_ghosts(pack, tiles, ghost_ids, ghosts)


def derivative_kernel(wide, tall, deep, table):
    lane = lax.broadcasted_iota(jnp.int32, (ROWS, LANES), 1)
    column_x = jnp.zeros((ROWS, LANES), jnp.int32)
    for step in range(1, wide):
        column_x = column_x + (lane >= step * tall).astype(jnp.int32)
    column_y = lane - column_x * tall
    gap_x = lax.axis_index("gx") - column_x
    gap_y = lax.axis_index("gy") - column_y
    far = (jnp.maximum(jnp.abs(gap_x), jnp.abs(gap_y)) >= 3) & (lane < wide * tall)
    weight = jnp.where(far, 1.0, 0.0)
    middle_z = slab_middle(deep)[2]
    r = (gap_x.astype(f32), gap_y.astype(f32), jnp.full((ROWS, LANES), middle_z - 0.5, f32))
    square = r[0] * r[0] + r[1] * r[1] + r[2] * r[2] + core_sq
    inverse = 1.0 / square
    taylor = {(0, 0, 0): lax.rsqrt(square)}
    for spot, triple in enumerate(POWERS):
        degree = sum(triple)
        if degree > 0:
            once, twice = None, None
            for axis in range(3):
                down = list(triple)
                down[axis] -= 1
                if down[axis] >= 0:
                    term = r[axis] * taylor[tuple(down)]
                    once = term if once is None else once + term
                down[axis] -= 1
                if down[axis] >= 0:
                    term = taylor[tuple(down)]
                    twice = term if twice is None else twice + term
            total = once * (-(2.0 * degree - 1.0) / degree)
            if twice is not None:
                total = total - twice * ((degree - 1.0) / degree)
            taylor[triple] = total * inverse
        scaled = taylor[triple] * weight * FACTORIAL[spot]
        table[spot : spot + 1, :] = scaled[0:1, :]


def split_three(value):
    first = value.astype(bf16).astype(f32)
    rest = value - first
    second = rest.astype(bf16).astype(f32)
    return first, second, rest - second


def join(upper, lower):
    return jnp.where(row_ids() < 4, upper, pltpu.roll(lower, 4, 0))


def store_features(place, ref, parts):
    ref[pl.ds(pl.multiple_of(place * FEATURES, FEATURES), FEATURES), :] = jnp.concatenate(
        parts, axis=0
    ).astype(bf16)


def squares_in_row_three(value):
    square = value * value
    return pltpu.roll(square, 1, 0) + pltpu.roll(square, 2, 0) + pltpu.roll(square, 3, 0)


def centred(tile, middle):
    row = row_ids()
    shift = jnp.where(row == 0, middle[0], jnp.where(row == 1, middle[1], middle[2]))
    return jnp.where(row < 3, tile - shift, 0.0)


def source_features(tile, middle, place, sources, pushes):
    row = row_ids()
    here = centred(tile, middle)
    here = jnp.where(row == 3, squares_in_row_three(here) + core_sq, here)
    one, two, three = split_three(here)
    ones = jnp.where(row < 3, 1.0, 0.0)
    store_features(place, sources, [join(one, one), join(two, two), join(one, three), ones])
    push = jnp.where(row >= 4, tile, 0.0)
    one, two, three = split_three(push)
    lines = jnp.concatenate([pltpu.roll(one, 4, 0) + two, pltpu.roll(three, 4, 0)], axis=0).astype(bf16)
    spot = pl.ds(pl.multiple_of(place * 2 * ROWS, 2 * ROWS), 2 * ROWS)
    pushes[spot, 0:LANES] = lines
    pushes[spot, LANES : 2 * LANES] = lines


def target_features(tile, middle, place, targets):
    row = row_ids()
    here = centred(tile, middle)
    size = squares_in_row_three(here)
    one, two, three = split_three(jnp.where(row == 3, 1.0, here * -2.0))
    first, second, third = split_three(size)
    sizes = jnp.where(
        row == 0,
        pltpu.roll(first, 5, 0),
        jnp.where(row == 1, pltpu.roll(second, 6, 0), pltpu.roll(third, 7, 0)),
    )
    sizes = jnp.where(row < 3, sizes, 0.0)
    store_features(place, targets, [join(one, two), join(one, two), join(three, one), sizes])


def step_kernel(
    tiles, ghost_tiles, wide, tall, deep, beside, final, capacity,
    pair_targets, pair_sources, owners, pack, received, table, ghost_ids, *rest,
):
    devices = wide * tall * deep
    columns = wide * tall
    ghost_in = rest[: 2 * len(beside)]
    rest = rest[2 * len(beside) :]
    if final:
        sent, pack_out, speed, sources, targets, pushes, near, work, expansion, square, slots, counts = rest
    else:
        pack_out, leaf, ghosts, speed, sources, targets, pushes, near, work, expansion, square, line = rest
    row = row_ids()
    middle = slab_middle(deep)

    square[...] = jnp.zeros_like(square)
    work[...] = jnp.zeros_like(work)
    for k in range(3):
        total = received[pl.ds(k, columns, stride=4 * deep), :]
        for slab in range(1, deep):
            total = total + received[pl.ds(slab * 4 + k, columns, stride=4 * deep), :]
        square[0:columns, :] = total
        turned = square[...].T[0:TERMS, :]
        work[pl.ds(k, TERMS, stride=ROWS), :] = turned
        work[pl.ds(k + 4, TERMS, stride=ROWS), :] = turned
    for spot, outer in enumerate(POWERS):
        total = None
        for inner_spot, inner in enumerate(POWERS):
            if sum(outer) + sum(inner) > ORDER:
                continue
            merged = tuple(o + i for o, i in zip(outer, inner))
            term = spread(table, PLACE[merged]) * work[inner_spot * ROWS : (inner_spot + 1) * ROWS, :]
            total = term if total is None else total + term
        summed = jnp.sum(total, axis=1, keepdims=True) * (1.0 / FACTORIAL[spot])
        expansion[spot * ROWS : (spot + 1) * ROWS, :] = jnp.broadcast_to(summed, (ROWS, LANES))

    def evaluate(pair, carry):
        x, y, z = relative_pair(pack, pair, middle)
        over_x = None
        for a in range(ORDER, -1, -1):
            over_y = None
            for b in range(ORDER - a, -1, -1):
                over_z = None
                for c in range(ORDER - a - b, -1, -1):
                    spot = PLACE[a, b, c]
                    factor = expansion[spot * ROWS : (spot + 1) * ROWS, :]
                    over_z = factor if over_z is None else over_z * z + factor
                over_y = over_z if over_y is None else over_y * y + over_z
            over_x = over_y if over_x is None else over_x * x + over_y
        spot = pl.multiple_of(pair * (2 * ROWS), 2 * ROWS)
        speed[pl.ds(spot, ROWS), :] = over_x
        speed[pl.ds(spot + ROWS, ROWS), :] = pltpu.roll(over_x, 4, 0)
        return carry

    lax.fori_loop(0, tiles // 2, evaluate, 0)

    def own_tile(tile, carry):
        value = tile_of(pack, tile)
        source_features(value, middle, tile, sources, pushes)
        target_features(value, middle, tile, targets)
        return carry

    lax.fori_loop(0, tiles, own_tile, 0, unroll=2)
    for number, (name, count) in enumerate(beside):
        index = lax.axis_index(name)
        odd = lax.rem(index, 2) == 1
        has_lower, has_upper = index > 0, index < count - 1
        from_a, from_b = ghost_in[2 * number], ghost_in[2 * number + 1]

        def ghost_tile(tile, carry, number=number, odd=odd, lows=has_lower, ups=has_upper, a=from_a, b=from_b):
            one, other = tile_of(a, tile), tile_of(b, tile)
            base = tiles + 2 * number * ghost_tiles + tile
            for which, (value, present) in enumerate(
                ((jnp.where(odd, one, other), lows), (jnp.where(odd, other, one), ups))
            ):
                value = jnp.where((row < 4) | present, value, 0.0)
                source_features(value, middle, base + which * ghost_tiles, sources, pushes)
            return carry

        lax.fori_loop(0, ghost_tiles, ghost_tile, 0)

    near[...] = jnp.zeros_like(near)
    pair_count = pair_targets.shape[0]
    batch = BATCH if pair_count % BATCH == 0 else 1

    def batch_of_pairs(number, carry):
        names = [(pair_targets[number * batch + at], pair_sources[number * batch + at]) for at in range(batch)]
        gaps = [
            lax.dot_general(
                sources[pl.ds(pl.multiple_of(there * FEATURES, FEATURES), FEATURES), :],
                targets[pl.ds(pl.multiple_of(here * FEATURES, FEATURES), FEATURES), :],
                (((0,), (0,)), ((), ())),
                preferred_element_type=f32,
            )
            for here, there in names
        ]
        weights = []
        for gap in gaps:
            kernel_block = lax.rsqrt(jnp.maximum(gap, core_sq))
            coarse = kernel_block.astype(bf16)
            fine = (kernel_block - coarse.astype(f32)).astype(bf16)
            weights.append(jnp.concatenate([coarse, fine], axis=0))
        gains = [
            jnp.dot(
                pushes[pl.ds(pl.multiple_of(there * 2 * ROWS, 2 * ROWS), 2 * ROWS), :],
                weight,
                preferred_element_type=f32,
            )
            for (here, there), weight in zip(names, weights)
        ]
        for (here, there), gain in zip(names, gains):
            spot = pl.ds(pl.multiple_of(here * 2 * ROWS, 2 * ROWS), 2 * ROWS)
            near[spot, :] = near[spot, :] + gain
        return carry

    lax.fori_loop(0, pair_count // batch, batch_of_pairs, 0)

    def advance(tile, carry):
        spot = pl.multiple_of(tile * 2 * ROWS, 2 * ROWS)
        upper, lower = near[pl.ds(spot, ROWS), :], near[pl.ds(spot + ROWS, ROWS), :]
        close = upper + pltpu.roll(upper, 4, 0) + lower
        velocity = jnp.where(row < 3, close + tile_of(speed, tile), 0.0)
        place = pl.ds(pl.multiple_of(tile * ROWS, ROWS), ROWS)
        speed[place, :] = velocity
        pack_out[place, :] = pack[place, :] + time_step * velocity
        return carry

    lax.fori_loop(0, tiles, advance, 0, unroll=4)

    if not final:
        leaf_moments(pack_out, tiles, devices, leaf, work, line)
        pick_ghosts(pack_out, tiles, ghost_ids, ghosts)
        return

    group = wide * tall
    blank = jnp.zeros((ROWS, LANES), f32)
    pack_out[tiles * ROWS : (tiles + 1) * ROWS, :] = blank
    speed[tiles * ROWS : (tiles + 1) * ROWS, :] = blank

    def clear_slot(at, carry):
        slots[at] = tiles
        return carry

    def clear_count(at, carry):
        counts[at] = 0
        return carry

    def assign(block, carry):
        owner = owners[block]
        earlier = counts[owner]
        counts[owner] = earlier + 1
        slots[owner * capacity + earlier] = block
        return carry

    lax.fori_loop(0, group * capacity, clear_slot, 0)
    lax.fori_loop(0, group, clear_count, 0)
    lax.fori_loop(0, tiles, assign, 0)
    for at in range(group * capacity):
        block = slots[at]
        sent[at * 6 : at * 6 + 3, :] = tile_of(pack_out, block)[0:3, :]
        sent[at * 6 + 3 : at * 6 + 6, :] = tile_of(speed, block)[0:3, :]


def swap_neighbours(block, name):
    count = lax.axis_size(name)
    if count == 1:
        return block, block
    even = [(i, i ^ 1) for i in range(count)]
    first = lax.ppermute(block, name, even)
    if count == 2:
        return first, first
    odd = [(i, (i + 1) % count if i % 2 else (i - 1) % count) for i in range(count)]
    return first, lax.ppermute(block, name, odd)


def per_device(offsets, strength, ghost_list, pair_targets, pair_sources, owners):
    wide, tall, deep = (lax.axis_size(name) for name in everywhere)
    devices, group = wide * tall * deep, wide * tall
    segments = offsets.shape[1]
    tiles = segments // LANES
    ghost_tiles = ghost_list.shape[0] // LANES
    capacity = max(2, 2 * tiles // group)
    ghost_ids = ghost_list.reshape(ghost_tiles, LANES)
    in_vmem = pl.BlockSpec(memory_space=pltpu.VMEM)
    in_smem = pl.BlockSpec(memory_space=pltpu.SMEM)
    pack_type = jax.ShapeDtypeStruct((tiles * ROWS, LANES), f32)
    leaf_type = jax.ShapeDtypeStruct((devices * 4, LANES), f32)
    ghost_type = jax.ShapeDtypeStruct((ghost_tiles * ROWS, LANES), f32)
    work = pltpu.VMEM((TERMS * ROWS, LANES), f32)
    line = pltpu.VMEM((ROWS, LANES), f32)
    params = pltpu.CompilerParams(vmem_limit_bytes=48 << 20)

    pack, leaf, ghosts = pl.pallas_call(
        functools.partial(prologue_kernel, tiles, devices, deep),
        out_shape=(pack_type, leaf_type, ghost_type),
        in_specs=[in_vmem] * 3,
        out_specs=(in_vmem,) * 3,
        scratch_shapes=[work, line],
        compiler_params=params,
        name="prologue",
    )(offsets, strength, ghost_ids)
    table = pl.pallas_call(
        functools.partial(derivative_kernel, wide, tall, deep),
        out_shape=jax.ShapeDtypeStruct((TERMS, LANES), f32),
        out_specs=in_vmem,
        compiler_params=params,
        name="derivatives",
    )()
    beside = tuple((name, lax.axis_size(name)) for name in everywhere)
    places = tiles + 2 * len(beside) * ghost_tiles
    scratch = [
        pltpu.VMEM((places * FEATURES, LANES), bf16),
        pltpu.VMEM((tiles * FEATURES, LANES), bf16),
        pltpu.VMEM((places * 2 * ROWS, 2 * LANES), bf16),
        pltpu.VMEM((tiles * 2 * ROWS, LANES), f32),
        work,
        work,
        pltpu.VMEM((LANES, LANES), f32),
    ]
    taller = pltpu.VMEM(((tiles + 1) * ROWS, LANES), f32)
    for step_number in range(2):
        final = step_number == 1
        received = lax.all_to_all(leaf, everywhere, split_axis=0, concat_axis=0, tiled=True)
        arrived = []
        for name, count in beside:
            arrived.extend(swap_neighbours(ghosts, name))
        if final:
            out_shape = jax.ShapeDtypeStruct((group * capacity * 6, LANES), f32)
            out_specs = in_vmem
            extra = [taller, taller] + scratch + [
                pltpu.SMEM((group * capacity,), jnp.int32),
                pltpu.SMEM((group,), jnp.int32),
            ]
        else:
            out_shape = (pack_type, leaf_type, ghost_type)
            out_specs = (in_vmem,) * 3
            extra = [taller] + scratch + [line]
        result = pl.pallas_call(
            functools.partial(
                step_kernel, tiles, ghost_tiles, wide, tall, deep, beside, final, capacity
            ),
            out_shape=out_shape,
            in_specs=[in_smem] * 3 + [in_vmem] * (4 + len(arrived)),
            out_specs=out_specs,
            scratch_shapes=extra,
            compiler_params=params,
            name="last_step" if final else "step",
        )(pair_targets, pair_sources, owners[:, 0], pack, received, table, ghost_ids, *arrived)
        if not final:
            pack, leaf, ghosts = result
    handed = lax.all_to_all(result, ("gx", "gy"), split_axis=0, concat_axis=0, tiled=True)
    handed = handed.reshape(group * capacity, 6, LANES)
    return (handed[:, :3], handed[:, 3:])


def solution(mesh):
    return jax.shard_map(
        per_device,
        mesh=mesh,
        in_specs=(
            P(None, everywhere),
            P(None, everywhere),
            P(everywhere),
            P(everywhere),
            P(everywhere),
            P(everywhere, None),
        ),
        out_specs=(P(everywhere, None, None), P(everywhere, None, None)),
        check_vma=False,
    )
```

```python
import functools
import math

import jax
import jax.numpy as jnp
import numpy as np
from jax import lax
from jax.experimental import pallas as pl
from jax.experimental.pallas import tpu as pltpu
from jax.sharding import PartitionSpec as P


ORDER = 5
LANES = 128
ROWS = 8
FEATURES = 32
BATCH = 16

core_sq = 0.0025
time_step = 0.1
everywhere = ("gx", "gy", "gz")
f32 = jnp.float32
bf16 = jnp.bfloat16


def exponents():
    entries = []
    for degree in range(ORDER + 1):
        for leading in range(degree, -1, -1):
            for middle in range(degree - leading, -1, -1):
                entries.append((leading, middle, degree - leading - middle))
    return entries


POWERS = exponents()
TERMS = len(POWERS)
PLACE = {triple: spot for spot, triple in enumerate(POWERS)}
FACTORIAL = [float(np.prod([math.factorial(e) for e in triple])) for triple in POWERS]


def row_ids():
    return lax.broadcasted_iota(jnp.int32, (ROWS, LANES), 0)


def spread(ref, row):
    return ref[pl.ds(row, ROWS, stride=0), :]


def tile_of(ref, tile):
    return ref[pl.ds(pl.multiple_of(tile * ROWS, ROWS), ROWS), :]


def slab_middle(deep):
    side_z = 1.0 / deep
    middle_x = lax.axis_index("gx").astype(f32) + 0.5
    middle_y = lax.axis_index("gy").astype(f32) + 0.5
    middle_z = lax.axis_index("gz").astype(f32) * side_z + 0.5 * side_z
    return middle_x, middle_y, middle_z


def relative_pair(pack, pair, middle):
    low = row_ids() < 4
    base = pair * (2 * ROWS)
    return [
        jnp.where(low, spread(pack, base + axis), spread(pack, base + ROWS + axis)) - middle[axis]
        for axis in range(3)
    ]


def moments_kernel(tiles, devices, pack, leaf, work, line):
    middle_x, middle_y, _ = slab_middle(1)
    middle = (middle_x, middle_y, 0.5)
    low = row_ids() < 4

    def accumulate(chosen):
        def body(pair, sums):
            x, y, z = relative_pair(pack, pair, middle)
            even, odd = tile_of(pack, 2 * pair), tile_of(pack, 2 * pair + 1)
            first = jnp.where(low, pltpu.roll(even, 4, 0), odd)
            value = {(0, 0, 0): first}
            gained = []
            for a in range(ORDER + 1):
                if a > 0:
                    value[a, 0, 0] = value[a - 1, 0, 0] * x
                if a not in chosen:
                    continue
                for b in range(ORDER + 1 - a):
                    if b > 0:
                        value[a, b, 0] = value[a, b - 1, 0] * y
                    for c in range(ORDER + 1 - a - b):
                        if c > 0:
                            value[a, b, c] = value[a, b, c - 1] * z
                        gained.append(value[a, b, c])
            return tuple(total + more for total, more in zip(sums, gained))

        names = [
            (a, b, c)
            for a in chosen
            for b in range(ORDER + 1 - a)
            for c in range(ORDER + 1 - a - b)
        ]
        zero = jnp.zeros((ROWS, LANES), f32)
        sums = lax.fori_loop(0, tiles // 2, body, tuple(zero for _ in names), unroll=4)
        for name, total in zip(names, sums):
            spot = PLACE[name]
            factor = (-1.0) ** sum(name) / FACTORIAL[spot]
            work[spot * ROWS : (spot + 1) * ROWS, :] = total * factor

    accumulate((0,))
    accumulate((1, 2, 3, 4, 5))
    line[...] = jnp.zeros_like(line)
    for k in range(3):
        both = work[pl.ds(k, TERMS, stride=ROWS), :] + work[pl.ds(k + 4, TERMS, stride=ROWS), :]
        summed = jnp.sum(both.T, axis=0, keepdims=True)
        line[k : k + 1, 0:TERMS] = summed
        line[k + 4 : k + 5, 0:TERMS] = summed
    copies = line[...]
    for at in range(devices * 4 // ROWS):
        leaf[at * ROWS : (at + 1) * ROWS, :] = copies


def pick_ghosts(pack, tiles, ghost_ids, ghosts):
    for out_tile in range(ghost_ids.shape[0]):
        wanted = jnp.broadcast_to(ghost_ids[out_tile : out_tile + 1, :], (ROWS, LANES))
        lane, owner = wanted & (LANES - 1), wanted >> 7
        found = jnp.zeros((ROWS, LANES), f32)
        for tile in range(tiles):
            moved = jnp.take_along_axis(
                pack[tile * ROWS : (tile + 1) * ROWS, :], lane, axis=1, mode="promise_in_bounds"
            )
            found = jnp.where(owner == tile, moved, found)
        ghosts[out_tile * ROWS : (out_tile + 1) * ROWS, :] = found


def prologue_kernel(tiles, deep, offsets_in, strength_in, ids_in, pack, ghosts, offsets, strength, ghost_ids, arrivals):
    loads = [
        pltpu.make_async_copy(source, target, arrivals.at[number])
        for number, (source, target) in enumerate(
            ((offsets_in, offsets), (strength_in, strength), (ids_in, ghost_ids))
        )
    ]
    for load in loads:
        load.start()
    side_z = 1.0 / deep
    axis = lax.broadcasted_iota(jnp.int32, (3, LANES), 0)
    corner = jnp.where(
        axis == 0,
        lax.axis_index("gx").astype(f32),
        jnp.where(
            axis == 1, lax.axis_index("gy").astype(f32), lax.axis_index("gz").astype(f32) * side_z
        ),
    )
    sides = jnp.where(axis == 2, side_z, 1.0)
    blank = jnp.zeros((1, LANES), f32)
    for load in loads:
        load.wait()
    for tile in range(tiles):
        span = slice(tile * LANES, (tile + 1) * LANES)
        base = tile * ROWS
        pack[base : base + 3, :] = corner + offsets[:, span] * sides
        pack[base + 3 : base + 4, :] = blank
        pack[base + 4 : base + 7, :] = strength[:, span]
        pack[base + 7 : base + 8, :] = blank
    pick_ghosts(pack, tiles, ghost_ids, ghosts)


def derivative_kernel(wide, tall, deep, table):
    lane = lax.broadcasted_iota(jnp.int32, (ROWS, LANES), 1)
    column_x = jnp.zeros((ROWS, LANES), jnp.int32)
    for step in range(1, wide):
        column_x = column_x + (lane >= step * tall).astype(jnp.int32)
    column_y = lane - column_x * tall
    gap_x = lax.axis_index("gx") - column_x
    gap_y = lax.axis_index("gy") - column_y
    far = (jnp.maximum(jnp.abs(gap_x), jnp.abs(gap_y)) >= 3) & (lane < wide * tall)
    weight = jnp.where(far, 1.0, 0.0)
    middle_z = slab_middle(deep)[2]
    r = (gap_x.astype(f32), gap_y.astype(f32), jnp.full((ROWS, LANES), middle_z - 0.5, f32))
    square = r[0] * r[0] + r[1] * r[1] + r[2] * r[2] + core_sq
    inverse = 1.0 / square
    taylor = {(0, 0, 0): lax.rsqrt(square)}
    for spot, triple in enumerate(POWERS):
        degree = sum(triple)
        if degree > 0:
            once, twice = None, None
            for axis in range(3):
                down = list(triple)
                down[axis] -= 1
                if down[axis] >= 0:
                    term = r[axis] * taylor[tuple(down)]
                    once = term if once is None else once + term
                down[axis] -= 1
                if down[axis] >= 0:
                    term = taylor[tuple(down)]
                    twice = term if twice is None else twice + term
            total = once * (-(2.0 * degree - 1.0) / degree)
            if twice is not None:
                total = total - twice * ((degree - 1.0) / degree)
            taylor[triple] = total * inverse
        scaled = taylor[triple] * weight * FACTORIAL[spot]
        table[spot : spot + 1, :] = scaled[0:1, :]


def split_three(value):
    first = value.astype(bf16).astype(f32)
    rest = value - first
    second = rest.astype(bf16).astype(f32)
    return first, second, rest - second


def join(upper, lower):
    return jnp.where(row_ids() < 4, upper, pltpu.roll(lower, 4, 0))


def store_features(place, ref, parts):
    ref[pl.ds(pl.multiple_of(place * FEATURES, FEATURES), FEATURES), :] = jnp.concatenate(
        parts, axis=0
    ).astype(bf16)


def squares_in_row_three(value):
    square = value * value
    return pltpu.roll(square, 1, 0) + pltpu.roll(square, 2, 0) + pltpu.roll(square, 3, 0)


def centred(tile, middle):
    row = row_ids()
    shift = jnp.where(row == 0, middle[0], jnp.where(row == 1, middle[1], middle[2]))
    return jnp.where(row < 3, tile - shift, 0.0)


def source_features(tile, middle, place, sources, pushes):
    row = row_ids()
    here = centred(tile, middle)
    here = jnp.where(row == 3, squares_in_row_three(here) + core_sq, here)
    one, two, three = split_three(here)
    ones = jnp.where(row < 3, 1.0, 0.0)
    store_features(place, sources, [join(one, one), join(two, two), join(one, three), ones])
    push = jnp.where(row >= 4, tile, 0.0)
    one, two, three = split_three(push)
    lines = jnp.concatenate([pltpu.roll(one, 4, 0) + two, pltpu.roll(three, 4, 0)], axis=0).astype(bf16)
    spot = pl.ds(pl.multiple_of(place * 2 * ROWS, 2 * ROWS), 2 * ROWS)
    pushes[spot, 0:LANES] = lines
    pushes[spot, LANES : 2 * LANES] = lines


def target_features(tile, middle, place, targets):
    row = row_ids()
    here = centred(tile, middle)
    size = squares_in_row_three(here)
    one, two, three = split_three(jnp.where(row == 3, 1.0, here * -2.0))
    first, second, third = split_three(size)
    sizes = jnp.where(
        row == 0,
        pltpu.roll(first, 5, 0),
        jnp.where(row == 1, pltpu.roll(second, 6, 0), pltpu.roll(third, 7, 0)),
    )
    sizes = jnp.where(row < 3, sizes, 0.0)
    store_features(place, targets, [join(one, two), join(one, two), join(three, one), sizes])


def near_kernel(tiles, ghost_tiles, deep, beside, pair_targets, pair_sources, pack, *rest):
    ghost_in = rest[: 2 * len(beside)]
    close, sources, targets, pushes, near = rest[2 * len(beside) :]
    row = row_ids()
    middle = slab_middle(deep)

    def own_tile(tile, carry):
        value = tile_of(pack, tile)
        source_features(value, middle, tile, sources, pushes)
        target_features(value, middle, tile, targets)
        return carry

    lax.fori_loop(0, tiles, own_tile, 0, unroll=2)
    for number, (name, count) in enumerate(beside):
        index = lax.axis_index(name)
        odd = lax.rem(index, 2) == 1
        has_lower, has_upper = index > 0, index < count - 1
        from_a, from_b = ghost_in[2 * number], ghost_in[2 * number + 1]

        def ghost_tile(tile, carry, number=number, odd=odd, lows=has_lower, ups=has_upper, a=from_a, b=from_b):
            one, other = tile_of(a, tile), tile_of(b, tile)
            base = tiles + 2 * number * ghost_tiles + tile
            for which, (value, present) in enumerate(
                ((jnp.where(odd, one, other), lows), (jnp.where(odd, other, one), ups))
            ):
                value = jnp.where((row < 4) | present, value, 0.0)
                source_features(value, middle, base + which * ghost_tiles, sources, pushes)
            return carry

        lax.fori_loop(0, ghost_tiles, ghost_tile, 0)

    near[...] = jnp.zeros_like(near)
    pair_count = pair_targets.shape[0]
    batch = BATCH if pair_count % BATCH == 0 else 1

    def batch_of_pairs(number, carry):
        names = [(pair_targets[number * batch + at], pair_sources[number * batch + at]) for at in range(batch)]
        gaps = [
            lax.dot_general(
                sources[pl.ds(pl.multiple_of(there * FEATURES, FEATURES), FEATURES), :],
                targets[pl.ds(pl.multiple_of(here * FEATURES, FEATURES), FEATURES), :],
                (((0,), (0,)), ((), ())),
                preferred_element_type=f32,
            )
            for here, there in names
        ]
        weights = []
        for gap in gaps:
            kernel_block = lax.rsqrt(jnp.maximum(gap, core_sq))
            coarse = kernel_block.astype(bf16)
            fine = (kernel_block - coarse.astype(f32)).astype(bf16)
            weights.append(jnp.concatenate([coarse, fine], axis=0))
        gains = [
            jnp.dot(
                pushes[pl.ds(pl.multiple_of(there * 2 * ROWS, 2 * ROWS), 2 * ROWS), :],
                weight,
                preferred_element_type=f32,
            )
            for (here, there), weight in zip(names, weights)
        ]
        for (here, there), gain in zip(names, gains):
            spot = pl.ds(pl.multiple_of(here * 2 * ROWS, 2 * ROWS), 2 * ROWS)
            near[spot, :] = near[spot, :] + gain
        return carry

    lax.fori_loop(0, pair_count // batch, batch_of_pairs, 0)

    def collect(tile, carry):
        spot = pl.multiple_of(tile * 2 * ROWS, 2 * ROWS)
        upper, lower = near[pl.ds(spot, ROWS), :], near[pl.ds(spot + ROWS, ROWS), :]
        close[pl.ds(pl.multiple_of(tile * ROWS, ROWS), ROWS), :] = upper + pltpu.roll(upper, 4, 0) + lower
        return carry

    lax.fori_loop(0, tiles, collect, 0, unroll=4)


def far_kernel(tiles, wide, tall, deep, final, capacity, chosen, pack, close, received, table, *rest):
    columns = wide * tall
    if final:
        owners = chosen
        sent, pack_out, speed, work, expansion, square, slots, counts = rest
    else:
        ghost_ids = chosen
        pack_out, ghosts, speed, work, expansion, square = rest
    row = row_ids()
    middle = slab_middle(deep)

    square[...] = jnp.zeros_like(square)
    work[...] = jnp.zeros_like(work)
    for k in range(3):
        total = received[pl.ds(k, columns, stride=4 * deep), :]
        for slab in range(1, deep):
            total = total + received[pl.ds(slab * 4 + k, columns, stride=4 * deep), :]
        square[0:columns, :] = total
        turned = square[...].T[0:TERMS, :]
        work[pl.ds(k, TERMS, stride=ROWS), :] = turned
        work[pl.ds(k + 4, TERMS, stride=ROWS), :] = turned
    for spot, outer in enumerate(POWERS):
        total = None
        for inner_spot, inner in enumerate(POWERS):
            if sum(outer) + sum(inner) > ORDER:
                continue
            merged = tuple(o + i for o, i in zip(outer, inner))
            term = spread(table, PLACE[merged]) * work[inner_spot * ROWS : (inner_spot + 1) * ROWS, :]
            total = term if total is None else total + term
        summed = jnp.sum(total, axis=1, keepdims=True) * (1.0 / FACTORIAL[spot])
        expansion[spot * ROWS : (spot + 1) * ROWS, :] = jnp.broadcast_to(summed, (ROWS, LANES))

    def evaluate(pair, carry):
        x, y, z = relative_pair(pack, pair, middle)
        over_x = None
        for a in range(ORDER, -1, -1):
            over_y = None
            for b in range(ORDER - a, -1, -1):
                over_z = None
                for c in range(ORDER - a - b, -1, -1):
                    spot = PLACE[a, b, c]
                    factor = expansion[spot * ROWS : (spot + 1) * ROWS, :]
                    over_z = factor if over_z is None else over_z * z + factor
                over_y = over_z if over_y is None else over_y * y + over_z
            over_x = over_y if over_x is None else over_x * x + over_y
        spot = pl.multiple_of(pair * (2 * ROWS), 2 * ROWS)
        speed[pl.ds(spot, ROWS), :] = over_x
        speed[pl.ds(spot + ROWS, ROWS), :] = pltpu.roll(over_x, 4, 0)
        return carry

    lax.fori_loop(0, tiles // 2, evaluate, 0, unroll=4)

    def advance(tile, carry):
        place = pl.ds(pl.multiple_of(tile * ROWS, ROWS), ROWS)
        velocity = jnp.where(row < 3, close[place, :] + speed[place, :], 0.0)
        speed[place, :] = velocity
        pack_out[place, :] = pack[place, :] + time_step * velocity
        return carry

    lax.fori_loop(0, tiles, advance, 0, unroll=4)

    if not final:
        pick_ghosts(pack_out, tiles, ghost_ids, ghosts)
        return

    group = wide * tall
    blank = jnp.zeros((ROWS, LANES), f32)
    pack_out[tiles * ROWS : (tiles + 1) * ROWS, :] = blank
    speed[tiles * ROWS : (tiles + 1) * ROWS, :] = blank

    def clear_slot(at, carry):
        slots[at] = tiles
        return carry

    def clear_count(at, carry):
        counts[at] = 0
        return carry

    def assign(block, carry):
        owner = owners[block]
        earlier = counts[owner]
        counts[owner] = earlier + 1
        slots[owner * capacity + earlier] = block
        return carry

    lax.fori_loop(0, group * capacity, clear_slot, 0)
    lax.fori_loop(0, group, clear_count, 0)
    lax.fori_loop(0, tiles, assign, 0)
    for at in range(group * capacity):
        block = slots[at]
        sent[at * 6 : at * 6 + 3, :] = tile_of(pack_out, block)[0:3, :]
        sent[at * 6 + 3 : at * 6 + 6, :] = tile_of(speed, block)[0:3, :]


def receive_kernel(handed, positions, velocity):
    count = positions.shape[1]
    for axis in range(3):
        positions[axis] = handed[pl.ds(axis, count, stride=6), :]
        velocity[axis] = handed[pl.ds(axis + 3, count, stride=6), :]


def swap_neighbours(block, name):
    count = lax.axis_size(name)
    if count == 1:
        return block, block
    even = [(i, i ^ 1) for i in range(count)]
    first = lax.ppermute(block, name, even)
    if count == 2:
        return first, first
    deep = lax.axis_size("gz")
    if name != "gz" and deep % 2 == 0:
        odd = []
        for i in range(count):
            for k in range(deep):
                end = i in (0, count - 1)
                other = i * deep + (k ^ 1) if end else (i + 1 if i % 2 else i - 1) * deep + k
                odd.append((i * deep + k, other))
        return first, lax.ppermute(block, (name, "gz"), odd)
    odd = [(i, (i + 1) % count if i % 2 else (i - 1) % count) for i in range(count)]
    return first, lax.ppermute(block, name, odd)


def per_device(offsets, strength, ghost_list, pair_targets, pair_sources, owners):
    wide, tall, deep = (lax.axis_size(name) for name in everywhere)
    devices, group = wide * tall * deep, wide * tall
    segments = offsets.shape[1]
    tiles = segments // LANES
    ghost_tiles = ghost_list.shape[0] // LANES
    capacity = max(2, 2 * tiles // group)
    ghost_ids = ghost_list.reshape(ghost_tiles, LANES)
    in_vmem = pl.BlockSpec(memory_space=pltpu.VMEM)
    in_smem = pl.BlockSpec(memory_space=pltpu.SMEM)
    pack_type = jax.ShapeDtypeStruct((tiles * ROWS, LANES), f32)
    leaf_type = jax.ShapeDtypeStruct((devices * 4, LANES), f32)
    ghost_type = jax.ShapeDtypeStruct((ghost_tiles * ROWS, LANES), f32)
    work = pltpu.VMEM((TERMS * ROWS, LANES), f32)
    line = pltpu.VMEM((ROWS, LANES), f32)
    params = pltpu.CompilerParams(vmem_limit_bytes=48 << 20)

    in_place = pl.BlockSpec(memory_space=pltpu.HBM)

    pack, ghosts = pl.pallas_call(
        functools.partial(prologue_kernel, tiles, deep),
        out_shape=(pack_type, ghost_type),
        in_specs=[in_place] * 3,
        out_specs=(in_vmem,) * 2,
        scratch_shapes=[
            pltpu.VMEM(offsets.shape, f32),
            pltpu.VMEM(strength.shape, f32),
            pltpu.VMEM(ghost_ids.shape, jnp.int32),
            pltpu.SemaphoreType.DMA((3,)),
        ],
        compiler_params=params,
        name="prologue",
    )(*(pltpu.with_memory_space_constraint(value, pltpu.HBM) for value in (offsets, strength, ghost_ids)))
    table = pl.pallas_call(
        functools.partial(derivative_kernel, wide, tall, deep),
        out_shape=jax.ShapeDtypeStruct((TERMS, LANES), f32),
        out_specs=in_vmem,
        compiler_params=params,
        name="derivatives",
    )()
    beside = tuple((name, lax.axis_size(name)) for name in everywhere)
    places = tiles + 2 * len(beside) * ghost_tiles
    taller = pltpu.VMEM(((tiles + 1) * ROWS, LANES), f32)
    for step_number in range(2):
        final = step_number == 1
        arrived = []
        for name, count in beside:
            arrived.extend(swap_neighbours(ghosts, name))
        leaf = pl.pallas_call(
            functools.partial(moments_kernel, tiles, devices),
            out_shape=leaf_type,
            in_specs=[in_vmem],
            out_specs=in_vmem,
            scratch_shapes=[work, line],
            compiler_params=params,
            name="moments",
        )
        leaf = leaf(pack)
        received = lax.all_to_all(leaf, everywhere, split_axis=0, concat_axis=0, tiled=True)
        close = pl.pallas_call(
            functools.partial(near_kernel, tiles, ghost_tiles, deep, beside),
            out_shape=pack_type,
            in_specs=[in_smem] * 2 + [in_vmem] * (1 + len(arrived)),
            out_specs=in_vmem,
            scratch_shapes=[
                pltpu.VMEM((places * FEATURES, LANES), bf16),
                pltpu.VMEM((tiles * FEATURES, LANES), bf16),
                pltpu.VMEM((places * 2 * ROWS, 2 * LANES), bf16),
                pltpu.VMEM((tiles * 2 * ROWS, LANES), f32),
            ],
            compiler_params=params,
            name="near",
        )(pair_targets, pair_sources, pack, *arrived)
        if final:
            out_shape = jax.ShapeDtypeStruct((group * capacity * 6, LANES), f32)
            out_specs = in_vmem
            extra = [taller, taller, work, work, pltpu.VMEM((LANES, LANES), f32)] + [
                pltpu.SMEM((group * capacity,), jnp.int32),
                pltpu.SMEM((group,), jnp.int32),
            ]
        else:
            out_shape = (pack_type, ghost_type)
            out_specs = (in_vmem,) * 2
            extra = [taller, work, work, pltpu.VMEM((LANES, LANES), f32)]
        result = pl.pallas_call(
            functools.partial(far_kernel, tiles, wide, tall, deep, final, capacity),
            out_shape=out_shape,
            in_specs=[in_smem if final else in_vmem] + [in_vmem] * 4,
            out_specs=out_specs,
            scratch_shapes=extra,
            compiler_params=params,
            name="last_far" if final else "far",
        )(owners[:, 0] if final else ghost_ids, pack, close, received, table)
        if not final:
            pack, ghosts = result
    handed = lax.all_to_all(result, ("gx", "gy"), split_axis=0, concat_axis=0, tiled=True)
    moved = jax.ShapeDtypeStruct((3, group * capacity, LANES), f32)
    moved = pl.pallas_call(
        receive_kernel,
        out_shape=(moved, moved),
        in_specs=[in_vmem],
        out_specs=(in_vmem,) * 2,
        compiler_params=params,
        name="receive",
    )(handed)
    return tuple(value.transpose(1, 0, 2) for value in moved)


def solution(mesh):
    return jax.shard_map(
        per_device,
        mesh=mesh,
        in_specs=(
            P(None, everywhere),
            P(None, everywhere),
            P(everywhere),
            P(everywhere),
            P(everywhere),
            P(everywhere, None),
        ),
        out_specs=(P(everywhere, None, None), P(everywhere, None, None)),
        check_vma=False,
    )
```

```python
import functools
import math

import jax
import jax.numpy as jnp
import numpy as np
from jax import lax
from jax.experimental import pallas as pl
from jax.experimental.pallas import tpu as pltpu
from jax.sharding import PartitionSpec as P


ORDER = 5
LANES = 128
ROWS = 8
FEATURES = 32
BATCH = 128
LEAD = 12
LAG = 8

core_sq = 0.0025
time_step = 0.1
everywhere = ("gx", "gy", "gz")
f32 = jnp.float32
bf16 = jnp.bfloat16


def exponents():
    entries = []
    for degree in range(ORDER + 1):
        for leading in range(degree, -1, -1):
            for middle in range(degree - leading, -1, -1):
                entries.append((leading, middle, degree - leading - middle))
    return entries


POWERS = exponents()
TERMS = len(POWERS)
PLACE = {triple: spot for spot, triple in enumerate(POWERS)}
FACTORIAL = [float(np.prod([math.factorial(e) for e in triple])) for triple in POWERS]


def row_ids():
    return lax.broadcasted_iota(jnp.int32, (ROWS, LANES), 0)


def spread(ref, row):
    return ref[pl.ds(row, ROWS, stride=0), :]


def tile_of(ref, tile):
    return ref[pl.ds(pl.multiple_of(tile * ROWS, ROWS), ROWS), :]


def slab_middle(deep):
    side_z = 1.0 / deep
    middle_x = lax.axis_index("gx").astype(f32) + 0.5
    middle_y = lax.axis_index("gy").astype(f32) + 0.5
    middle_z = lax.axis_index("gz").astype(f32) * side_z + 0.5 * side_z
    return middle_x, middle_y, middle_z


def relative_pair(pack, pair, middle):
    low = row_ids() < 4
    base = pair * (2 * ROWS)
    return [
        jnp.where(low, spread(pack, base + axis), spread(pack, base + ROWS + axis)) - middle[axis]
        for axis in range(3)
    ]


def leaf_moments(pack, tiles, devices, copies, work, line):
    middle_x, middle_y, _ = slab_middle(1)
    middle = (middle_x, middle_y, 0.5)
    low = row_ids() < 4

    def accumulate(chosen):
        def body(pair, sums):
            x, y, z = relative_pair(pack, pair, middle)
            even, odd = tile_of(pack, 2 * pair), tile_of(pack, 2 * pair + 1)
            first = jnp.where(low, pltpu.roll(even, 4, 0), odd)
            value = {(0, 0, 0): first}
            gained = []
            for a in range(ORDER + 1):
                if a > 0:
                    value[a, 0, 0] = value[a - 1, 0, 0] * x
                if a not in chosen:
                    continue
                for b in range(ORDER + 1 - a):
                    if b > 0:
                        value[a, b, 0] = value[a, b - 1, 0] * y
                    for c in range(ORDER + 1 - a - b):
                        if c > 0:
                            value[a, b, c] = value[a, b, c - 1] * z
                        gained.append(value[a, b, c])
            return tuple(total + more for total, more in zip(sums, gained))

        names = [
            (a, b, c)
            for a in chosen
            for b in range(ORDER + 1 - a)
            for c in range(ORDER + 1 - a - b)
        ]
        zero = jnp.zeros((ROWS, LANES), f32)
        sums = lax.fori_loop(0, tiles // 2, body, tuple(zero for _ in names), unroll=4)
        for name, total in zip(names, sums):
            spot = PLACE[name]
            factor = (-1.0) ** sum(name) / FACTORIAL[spot]
            work[spot * ROWS : (spot + 1) * ROWS, :] = total * factor

    accumulate((0,))
    accumulate((1, 2, 3, 4, 5))
    line[...] = jnp.zeros_like(line)
    for k in range(3):
        both = work[pl.ds(k, TERMS, stride=ROWS), :] + work[pl.ds(k + 4, TERMS, stride=ROWS), :]
        summed = jnp.sum(both.T, axis=0, keepdims=True)
        line[k : k + 1, 0:TERMS] = summed
        line[k + 4 : k + 5, 0:TERMS] = summed
    both = line[...]
    for at in range(devices * 4 // ROWS):
        copies[at * ROWS : (at + 1) * ROWS, :] = both


def pick_ghosts(pack, tiles, ghost_ids, ghosts):
    for out_tile in range(ghost_ids.shape[0]):
        wanted = jnp.broadcast_to(ghost_ids[out_tile : out_tile + 1, :], (ROWS, LANES))
        lane, owner = wanted & (LANES - 1), wanted >> 7
        found = jnp.zeros((ROWS, LANES), f32)
        for tile in range(tiles):
            moved = jnp.take_along_axis(
                pack[tile * ROWS : (tile + 1) * ROWS, :], lane, axis=1, mode="promise_in_bounds"
            )
            found = jnp.where(owner == tile, moved, found)
        ghosts[out_tile * ROWS : (out_tile + 1) * ROWS, :] = found


def pick_positions(pack, tiles, ghost_ids, ghosts):
    low = row_ids() < 4
    pairs = ghost_ids.shape[0] // 2
    lanes, owner, found = [], [], []
    for pair in range(pairs):
        wanted = jnp.where(low, spread(ghost_ids, 2 * pair), spread(ghost_ids, 2 * pair + 1))
        lanes.append(wanted & (LANES - 1))
        owner.append(wanted >> 7)
        found.append(jnp.zeros((ROWS, LANES), f32))
    for tile in range(tiles):
        value = pack[tile * ROWS : (tile + 1) * ROWS, :]
        value = jnp.where(low, value, pltpu.roll(value, 4, 0))
        for pair in range(pairs):
            moved = jnp.take_along_axis(value, lanes[pair], axis=1, mode="promise_in_bounds")
            found[pair] = jnp.where(owner[pair] == tile, moved, found[pair])
    for pair in range(pairs):
        ghosts[pair * ROWS : (pair + 1) * ROWS, :] = found[pair]


def prologue_kernel(
    tiles, devices, deep, offsets_in, strength_in, ids_in, pack, ghosts, leaf,
    offsets, strength, ghost_ids, arrivals, copies, leaving, work, line,
):
    loads = [
        pltpu.make_async_copy(source, target, arrivals.at[number])
        for number, (source, target) in enumerate(
            ((offsets_in, offsets), (strength_in, strength), (ids_in, ghost_ids))
        )
    ]
    for load in loads:
        load.start()
    side_z = 1.0 / deep
    axis = lax.broadcasted_iota(jnp.int32, (3, LANES), 0)
    corner = jnp.where(
        axis == 0,
        lax.axis_index("gx").astype(f32),
        jnp.where(
            axis == 1, lax.axis_index("gy").astype(f32), lax.axis_index("gz").astype(f32) * side_z
        ),
    )
    sides = jnp.where(axis == 2, side_z, 1.0)
    blank = jnp.zeros((1, LANES), f32)
    for load in loads:
        load.wait()
    for tile in range(tiles):
        span = slice(tile * LANES, (tile + 1) * LANES)
        base = tile * ROWS
        pack[base : base + 3, :] = corner + offsets[:, span] * sides
        pack[base + 3 : base + 4, :] = blank
        pack[base + 4 : base + 7, :] = strength[:, span]
        pack[base + 7 : base + 8, :] = blank
    leaf_moments(pack, tiles, devices, copies, work, line)
    store = pltpu.make_async_copy(copies, leaf, leaving.at[0])
    store.start()
    pick_ghosts(pack, tiles, ghost_ids, ghosts)
    store.wait()


def derivative_kernel(wide, tall, deep, table):
    lane = lax.broadcasted_iota(jnp.int32, (ROWS, LANES), 1)
    column_x = jnp.zeros((ROWS, LANES), jnp.int32)
    for step in range(1, wide):
        column_x = column_x + (lane >= step * tall).astype(jnp.int32)
    column_y = lane - column_x * tall
    gap_x = lax.axis_index("gx") - column_x
    gap_y = lax.axis_index("gy") - column_y
    far = (jnp.maximum(jnp.abs(gap_x), jnp.abs(gap_y)) >= 3) & (lane < wide * tall)
    weight = jnp.where(far, 1.0, 0.0)
    middle_z = slab_middle(deep)[2]
    r = (gap_x.astype(f32), gap_y.astype(f32), jnp.full((ROWS, LANES), middle_z - 0.5, f32))
    square = r[0] * r[0] + r[1] * r[1] + r[2] * r[2] + core_sq
    inverse = 1.0 / square
    taylor = {(0, 0, 0): lax.rsqrt(square)}
    for spot, triple in enumerate(POWERS):
        degree = sum(triple)
        if degree > 0:
            once, twice = None, None
            for axis in range(3):
                down = list(triple)
                down[axis] -= 1
                if down[axis] >= 0:
                    term = r[axis] * taylor[tuple(down)]
                    once = term if once is None else once + term
                down[axis] -= 1
                if down[axis] >= 0:
                    term = taylor[tuple(down)]
                    twice = term if twice is None else twice + term
            total = once * (-(2.0 * degree - 1.0) / degree)
            if twice is not None:
                total = total - twice * ((degree - 1.0) / degree)
            taylor[triple] = total * inverse
        scaled = taylor[triple] * weight * FACTORIAL[spot]
        table[spot : spot + 1, :] = scaled[0:1, :]


def split_three(value):
    first = value.astype(bf16).astype(f32)
    rest = value - first
    second = rest.astype(bf16).astype(f32)
    return first, second, rest - second


def join(upper, lower):
    return jnp.where(row_ids() < 4, upper, pltpu.roll(lower, 4, 0))


def store_features(place, ref, parts):
    ref[pl.ds(pl.multiple_of(place * FEATURES, FEATURES), FEATURES), :] = jnp.concatenate(
        parts, axis=0
    ).astype(bf16)


def squares_in_row_three(value):
    square = value * value
    return pltpu.roll(square, 1, 0) + pltpu.roll(square, 2, 0) + pltpu.roll(square, 3, 0)


def centred(tile, middle):
    row = row_ids()
    shift = jnp.where(row == 0, middle[0], jnp.where(row == 1, middle[1], middle[2]))
    return jnp.where(row < 3, tile - shift, 0.0)


def source_features(tile, middle, place, sources, pushes):
    row = row_ids()
    here = centred(tile, middle)
    here = jnp.where(row == 3, squares_in_row_three(here) + core_sq, here)
    one, two, three = split_three(here)
    ones = jnp.where(row < 3, 1.0, 0.0)
    store_features(place, sources, [join(one, one), join(two, two), join(one, three), ones])
    push = jnp.where(row >= 4, tile, 0.0)
    one, two, three = split_three(push)
    lines = jnp.concatenate([pltpu.roll(one, 4, 0) + two, pltpu.roll(three, 4, 0)], axis=0).astype(bf16)
    spot = pl.ds(pl.multiple_of(place * 2 * ROWS, 2 * ROWS), 2 * ROWS)
    pushes[spot, 0:LANES] = lines
    pushes[spot, LANES : 2 * LANES] = lines


def target_features(tile, middle, place, targets):
    row = row_ids()
    here = centred(tile, middle)
    size = squares_in_row_three(here)
    one, two, three = split_three(jnp.where(row == 3, 1.0, here * -2.0))
    first, second, third = split_three(size)
    sizes = jnp.where(
        row == 0,
        pltpu.roll(first, 5, 0),
        jnp.where(row == 1, pltpu.roll(second, 6, 0), pltpu.roll(third, 7, 0)),
    )
    sizes = jnp.where(row < 3, sizes, 0.0)
    store_features(place, targets, [join(one, two), join(one, two), join(three, one), sizes])


def block_placer(owners, group, capacity):
    blocks = owners.shape[1]
    own = owners[...].astype(f32)
    down = lax.broadcasted_iota(jnp.int32, (blocks, blocks), 0)
    along = lax.broadcasted_iota(jnp.int32, (blocks, blocks), 1)
    wide = jnp.broadcast_to(own, (blocks, blocks))
    tall = jnp.sum(jnp.where(down == along, wide, 0.0), axis=1, keepdims=True)
    earlier = jnp.where((wide == tall) & (down < along), 1.0, 0.0)
    slot = own * float(capacity) + jnp.sum(earlier, axis=0, keepdims=True)
    place = lax.broadcasted_iota(jnp.int32, (group * capacity, blocks), 0).astype(f32)
    return jnp.where(place == slot, 1.0, 0.0).astype(bf16)


def near_kernel(
    tiles, ghost_tiles, deep, beside, targets_in, sources_in, pack, *rest
):
    count = 2 * len(beside)
    ghost_in, strength_in, rest = rest[:count], rest[count : 2 * count], rest[2 * count :]
    halved = ghost_in[0].shape[0] < strength_in[0].shape[0]
    close, sources, targets, pushes, near, pair_targets, pair_sources, arrivals = rest
    loads = [
        pltpu.make_async_copy(source, target, arrivals.at[number])
        for number, (source, target) in enumerate(
            ((targets_in, pair_targets), (sources_in, pair_sources))
        )
    ]
    for load in loads:
        load.start()
    row = row_ids()
    middle = slab_middle(deep)

    def own_tile(tile, carry):
        value = tile_of(pack, tile)
        source_features(value, middle, tile, sources, pushes)
        target_features(value, middle, tile, targets)
        return carry

    lax.fori_loop(0, tiles, own_tile, 0, unroll=2)
    for number, (name, count) in enumerate(beside):
        index = lax.axis_index(name)
        odd = lax.rem(index, 2) == 1
        has_lower, has_upper = index > 0, index < count - 1

        def ghost_pair(pair, carry, number=number, odd=odd, lows=has_lower, ups=has_upper):
            for which, present in enumerate((lows, ups)):
                def held(refs, tile):
                    one, other = tile_of(refs[2 * number], tile), tile_of(refs[2 * number + 1], tile)
                    return jnp.where(odd, other, one) if which else jnp.where(odd, one, other)

                base = tiles + (2 * number + which) * ghost_tiles
                if halved:
                    both = held(ghost_in, pair)
                for half in range(2):
                    tile = 2 * pair + half
                    value = held(strength_in, tile)
                    if halved:
                        value = jnp.where(row < 4, pltpu.roll(both, 4, 0) if half else both, value)
                    value = jnp.where((row < 4) | present, value, 0.0)
                    source_features(value, middle, base + tile, sources, pushes)
            return carry

        lax.fori_loop(0, ghost_tiles // 2, ghost_pair, 0)

    near[...] = jnp.zeros_like(near)
    for load in loads:
        load.wait()
    pair_count = pair_targets.shape[0]
    batch = BATCH if pair_count % BATCH == 0 else 1

    def batch_of_pairs(number, carry):
        names = [(pair_targets[number * batch + at], pair_sources[number * batch + at]) for at in range(batch)]

        def gap_of(at):
            here, there = names[at]
            return lax.dot_general(
                sources[pl.ds(pl.multiple_of(there * FEATURES, FEATURES), FEATURES), :],
                targets[pl.ds(pl.multiple_of(here * FEATURES, FEATURES), FEATURES), :],
                (((0,), (0,)), ((), ())),
                preferred_element_type=f32,
            )

        def gain_of(at, gap):
            there = names[at][1]
            kernel_block = lax.rsqrt(jnp.maximum(gap, core_sq))
            coarse = kernel_block.astype(bf16)
            fine = (kernel_block - coarse.astype(f32)).astype(bf16)
            return jnp.dot(
                pushes[pl.ds(pl.multiple_of(there * 2 * ROWS, 2 * ROWS), 2 * ROWS), :],
                jnp.concatenate([coarse, fine], axis=0),
                preferred_element_type=f32,
            )

        def add(at, gain):
            spot = pl.ds(pl.multiple_of(names[at][0] * 2 * ROWS, 2 * ROWS), 2 * ROWS)
            near[spot, :] = near[spot, :] + gain

        gaps, gains = {}, {}
        for at in range(batch + LEAD + LAG):
            if at < batch:
                gaps[at] = gap_of(at)
            if 0 <= at - LEAD < batch:
                gains[at - LEAD] = gain_of(at - LEAD, gaps.pop(at - LEAD))
            if 0 <= at - LEAD - LAG < batch:
                add(at - LEAD - LAG, gains.pop(at - LEAD - LAG))
        return carry

    lax.fori_loop(0, pair_count // batch, batch_of_pairs, 0)

    def collect(tile, carry):
        spot = pl.multiple_of(tile * 2 * ROWS, 2 * ROWS)
        upper, lower = near[pl.ds(spot, ROWS), :], near[pl.ds(spot + ROWS, ROWS), :]
        close[pl.ds(pl.multiple_of(tile * ROWS, ROWS), ROWS), :] = upper + pltpu.roll(upper, 4, 0) + lower
        return carry

    lax.fori_loop(0, tiles, collect, 0, unroll=4)


def far_kernel(tiles, wide, tall, deep, final, capacity, chosen, pack, close, received, table, *rest):
    columns = wide * tall
    if final:
        sent, moved, speed, work, expansion, square, owners, arrival = rest
        load = pltpu.make_async_copy(chosen, owners, arrival.at[0])
        load.start()
    else:
        pack_out, ghosts, leaf, speed, work, expansion, square, copies, leaving, line = rest
    row = row_ids()
    middle = slab_middle(deep)

    square[...] = jnp.zeros_like(square)
    work[...] = jnp.zeros_like(work)
    for k in range(3):
        total = received[pl.ds(k, columns, stride=4 * deep), :]
        for slab in range(1, deep):
            total = total + received[pl.ds(slab * 4 + k, columns, stride=4 * deep), :]
        square[0:columns, :] = total
        turned = square[...].T[0:TERMS, :]
        work[pl.ds(k, TERMS, stride=ROWS), :] = turned
        work[pl.ds(k + 4, TERMS, stride=ROWS), :] = turned
    for spot, outer in enumerate(POWERS):
        total = None
        for inner_spot, inner in enumerate(POWERS):
            if sum(outer) + sum(inner) > ORDER:
                continue
            merged = tuple(o + i for o, i in zip(outer, inner))
            term = spread(table, PLACE[merged]) * work[inner_spot * ROWS : (inner_spot + 1) * ROWS, :]
            total = term if total is None else total + term
        summed = jnp.sum(total, axis=1, keepdims=True) * (1.0 / FACTORIAL[spot])
        expansion[spot * ROWS : (spot + 1) * ROWS, :] = jnp.broadcast_to(summed, (ROWS, LANES))

    def evaluate(pair, carry):
        x, y, z = relative_pair(pack, pair, middle)
        over_x = None
        for a in range(ORDER, -1, -1):
            over_y = None
            for b in range(ORDER - a, -1, -1):
                over_z = None
                for c in range(ORDER - a - b, -1, -1):
                    spot = PLACE[a, b, c]
                    factor = expansion[spot * ROWS : (spot + 1) * ROWS, :]
                    over_z = factor if over_z is None else over_z * z + factor
                over_y = over_z if over_y is None else over_y * y + over_z
            over_x = over_y if over_x is None else over_x * x + over_y
        spot = pl.multiple_of(pair * (2 * ROWS), 2 * ROWS)
        speed[pl.ds(spot, ROWS), :] = over_x
        speed[pl.ds(spot + ROWS, ROWS), :] = pltpu.roll(over_x, 4, 0)
        return carry

    lax.fori_loop(0, tiles // 2, evaluate, 0, unroll=4)

    def advance(tile, carry):
        place = pl.ds(pl.multiple_of(tile * ROWS, ROWS), ROWS)
        velocity = jnp.where(row < 3, close[place, :] + speed[place, :], 0.0)
        later = pack[place, :] + time_step * velocity
        if final:
            moved[place, :] = jnp.where(row < 3, later, pltpu.roll(velocity, 3, 0))
        else:
            pack_out[place, :] = later
        return carry

    lax.fori_loop(0, tiles, advance, 0, unroll=4)

    if not final:
        leaf_moments(pack_out, tiles, wide * tall * deep, copies, work, line)
        store = pltpu.make_async_copy(copies, leaf, leaving.at[0])
        store.start()
        pick_positions(pack_out, tiles, chosen, ghosts)
        store.wait()
        return

    group = wide * tall
    load.wait()
    placer = block_placer(owners, group, capacity)
    placer = jnp.concatenate([placer] * 3, axis=1)
    for field in range(6):
        values = split_three(moved[pl.ds(field, tiles, stride=ROWS), :])
        values = jnp.concatenate([value.astype(bf16) for value in values], axis=0)
        placed = jnp.dot(placer, values, preferred_element_type=f32)
        for owner in range(group):
            base = (owner * 6 + field) * capacity
            sent[base : base + capacity, :] = placed[owner * capacity : (owner + 1) * capacity, :]


def receive_kernel(capacity, handed, positions, velocity):
    for sender in range(positions.shape[1] // capacity):
        slots = slice(sender * capacity, (sender + 1) * capacity)
        for axis in range(3):
            base = (sender * 6 + axis) * capacity
            positions[axis, slots, :] = handed[base : base + capacity, :]
            base = base + 3 * capacity
            velocity[axis, slots, :] = handed[base : base + capacity, :]


def even_pairs(block, name):
    count = lax.axis_size(name)
    if count == 1:
        return block
    return lax.ppermute(block, name, [(i, i ^ 1) for i in range(count)])


def odd_pairs(block, name):
    count, deep = lax.axis_size(name), lax.axis_size("gz")
    if count <= 2:
        return block
    if name == "gz" or deep % 2:
        return lax.ppermute(
            block, name, [(i, (i + 1) % count if i % 2 else (i - 1) % count) for i in range(count)]
        )
    moves = []
    for i in range(count):
        for k in range(deep):
            end = i in (0, count - 1)
            other = i * deep + (k ^ 1) if end else (i + 1 if i % 2 else i - 1) * deep + k
            moves.append((i * deep + k, other))
    return lax.ppermute(block, (name, "gz"), moves)


def per_device(offsets, strength, ghost_list, pair_targets, pair_sources, owners):
    wide, tall, deep = (lax.axis_size(name) for name in everywhere)
    devices, group = wide * tall * deep, wide * tall
    segments = offsets.shape[1]
    tiles = segments // LANES
    ghost_tiles = ghost_list.shape[0] // LANES
    capacity = max(2, 2 * tiles // group)
    ghost_ids = ghost_list.reshape(ghost_tiles, LANES)
    in_vmem = pl.BlockSpec(memory_space=pltpu.VMEM)
    pack_type = jax.ShapeDtypeStruct((tiles * ROWS, LANES), f32)
    leaf_type = jax.ShapeDtypeStruct((devices * 4, LANES), f32)
    ghost_type = jax.ShapeDtypeStruct((ghost_tiles * ROWS, LANES), f32)
    work = pltpu.VMEM((TERMS * ROWS, LANES), f32)
    line = pltpu.VMEM((ROWS, LANES), f32)
    params = pltpu.CompilerParams(vmem_limit_bytes=48 << 20)

    in_place = pl.BlockSpec(memory_space=pltpu.HBM)
    in_hbm = functools.partial(pltpu.with_memory_space_constraint, memory_space=pltpu.HBM)

    copies = pltpu.VMEM((devices * 4, LANES), f32)
    one_copy = pltpu.SemaphoreType.DMA((1,))

    pack, ghosts, leaf = pl.pallas_call(
        functools.partial(prologue_kernel, tiles, devices, deep),
        out_shape=(pack_type, ghost_type, leaf_type),
        in_specs=[in_place] * 3,
        out_specs=(in_vmem, in_vmem, in_place),
        scratch_shapes=[
            pltpu.VMEM(offsets.shape, f32),
            pltpu.VMEM(strength.shape, f32),
            pltpu.VMEM(ghost_ids.shape, jnp.int32),
            pltpu.SemaphoreType.DMA((3,)),
            copies,
            one_copy,
            work,
            line,
        ],
        compiler_params=params,
        name="prologue",
    )(in_hbm(offsets), in_hbm(strength), in_hbm(ghost_ids))
    table = pl.pallas_call(
        functools.partial(derivative_kernel, wide, tall, deep),
        out_shape=jax.ShapeDtypeStruct((TERMS, LANES), f32),
        out_specs=in_vmem,
        compiler_params=params,
        name="derivatives",
    )()
    beside = tuple((name, lax.axis_size(name)) for name in everywhere)
    places = tiles + 2 * len(beside) * ghost_tiles
    for step_number in range(2):
        final = step_number == 1
        arrived = []
        for name, _ in beside:
            arrived.extend((even_pairs(ghosts, name), odd_pairs(ghosts, name)))
        if not final:
            strengths = arrived
        received = lax.all_to_all(leaf, everywhere, split_axis=0, concat_axis=0, tiled=True)
        close = pl.pallas_call(
            functools.partial(near_kernel, tiles, ghost_tiles, deep, beside),
            out_shape=pack_type,
            in_specs=[in_place] * 2 + [in_vmem] * (1 + 2 * len(arrived)),
            out_specs=in_vmem,
            scratch_shapes=[
                pltpu.VMEM((places * FEATURES, LANES), bf16),
                pltpu.VMEM((tiles * FEATURES, LANES), bf16),
                pltpu.VMEM((places * 2 * ROWS, 2 * LANES), bf16),
                pltpu.VMEM((tiles * 2 * ROWS, LANES), f32),
                pltpu.SMEM(pair_targets.shape, jnp.int32),
                pltpu.SMEM(pair_sources.shape, jnp.int32),
                pltpu.SemaphoreType.DMA((2,)),
            ],
            compiler_params=params,
            name="near",
        )(in_hbm(pair_targets), in_hbm(pair_sources), pack, *arrived, *strengths)
        speed, square = pltpu.VMEM((tiles * ROWS, LANES), f32), pltpu.VMEM((LANES, LANES), f32)
        if final:
            chosen = in_hbm(owners.reshape(1, tiles))
            out_shape = jax.ShapeDtypeStruct((group * capacity * 6, LANES), f32)
            out_specs = in_vmem
            extra = [
                pltpu.VMEM((tiles * ROWS, LANES), f32), speed, work, work, square,
                pltpu.VMEM((1, tiles), jnp.int32), one_copy,
            ]
        else:
            chosen = ghost_ids
            half_type = jax.ShapeDtypeStruct((ghost_tiles * 4, LANES), f32)
            out_shape = (pack_type, half_type, leaf_type)
            out_specs = (in_vmem, in_vmem, in_place)
            extra = [speed, work, work, square, copies, one_copy, line]
        result = pl.pallas_call(
            functools.partial(far_kernel, tiles, wide, tall, deep, final, capacity),
            out_shape=out_shape,
            in_specs=[in_place if final else in_vmem] + [in_vmem] * 4,
            out_specs=out_specs,
            scratch_shapes=extra,
            compiler_params=params,
            name="last_far" if final else "far",
        )(chosen, pack, close, received, table)
        if not final:
            pack, ghosts, leaf = result
    handed = lax.all_to_all(result, ("gx", "gy"), split_axis=0, concat_axis=0, tiled=True)
    moved = jax.ShapeDtypeStruct((3, group * capacity, LANES), f32)
    moved = pl.pallas_call(
        functools.partial(receive_kernel, capacity),
        out_shape=(moved, moved),
        in_specs=[in_vmem],
        out_specs=(in_vmem,) * 2,
        compiler_params=params,
        name="receive",
    )(handed)
    return tuple(value.transpose(1, 0, 2) for value in moved)


def solution(mesh):
    return jax.shard_map(
        per_device,
        mesh=mesh,
        in_specs=(
            P(None, everywhere),
            P(None, everywhere),
            P(everywhere),
            P(everywhere),
            P(everywhere),
            P(everywhere, None),
        ),
        out_specs=(P(everywhere, None, None), P(everywhere, None, None)),
        check_vma=False,
    )
```

```python
import functools
import math

import jax
import jax.numpy as jnp
import numpy as np
from jax import lax
from jax.experimental import pallas as pl
from jax.experimental.pallas import tpu as pltpu
from jax.sharding import PartitionSpec as P


ORDER = 5
LANES = 128
ROWS = 8
FEATURES = 32
BATCH = 128
LEAD = 12
LAG = 8

core_sq = 0.0025
time_step = 0.1
everywhere = ("gx", "gy", "gz")
f32 = jnp.float32
bf16 = jnp.bfloat16


def exponents():
    entries = []
    for degree in range(ORDER + 1):
        for leading in range(degree, -1, -1):
            for middle in range(degree - leading, -1, -1):
                entries.append((leading, middle, degree - leading - middle))
    return entries


POWERS = exponents()
TERMS = len(POWERS)
PLACE = {triple: spot for spot, triple in enumerate(POWERS)}
FACTORIAL = [float(np.prod([math.factorial(e) for e in triple])) for triple in POWERS]


def row_ids():
    return lax.broadcasted_iota(jnp.int32, (ROWS, LANES), 0)


def spread(ref, row):
    return ref[pl.ds(row, ROWS, stride=0), :]


def tile_of(ref, tile):
    return ref[pl.ds(pl.multiple_of(tile * ROWS, ROWS), ROWS), :]


def slab_middle(deep):
    side_z = 1.0 / deep
    middle_x = lax.axis_index("gx").astype(f32) + 0.5
    middle_y = lax.axis_index("gy").astype(f32) + 0.5
    middle_z = lax.axis_index("gz").astype(f32) * side_z + 0.5 * side_z
    return middle_x, middle_y, middle_z


def relative_pair(pack, pair, middle):
    low = row_ids() < 4
    base = pair * (2 * ROWS)
    return [
        jnp.where(low, spread(pack, base + axis), spread(pack, base + ROWS + axis)) - middle[axis]
        for axis in range(3)
    ]


def leaf_moments(pack, tiles, devices, copies, work, line):
    middle_x, middle_y, _ = slab_middle(1)
    middle = (middle_x, middle_y, 0.5)
    low = row_ids() < 4

    def accumulate(chosen):
        def body(pair, sums):
            x, y, z = relative_pair(pack, pair, middle)
            even, odd = tile_of(pack, 2 * pair), tile_of(pack, 2 * pair + 1)
            first = jnp.where(low, pltpu.roll(even, 4, 0), odd)
            value = {(0, 0, 0): first}
            gained = []
            for a in range(ORDER + 1):
                if a > 0:
                    value[a, 0, 0] = value[a - 1, 0, 0] * x
                if a not in chosen:
                    continue
                for b in range(ORDER + 1 - a):
                    if b > 0:
                        value[a, b, 0] = value[a, b - 1, 0] * y
                    for c in range(ORDER + 1 - a - b):
                        if c > 0:
                            value[a, b, c] = value[a, b, c - 1] * z
                        gained.append(value[a, b, c])
            return tuple(total + more for total, more in zip(sums, gained))

        names = [
            (a, b, c)
            for a in chosen
            for b in range(ORDER + 1 - a)
            for c in range(ORDER + 1 - a - b)
        ]
        zero = jnp.zeros((ROWS, LANES), f32)
        sums = lax.fori_loop(0, tiles // 2, body, tuple(zero for _ in names), unroll=4)
        for name, total in zip(names, sums):
            spot = PLACE[name]
            factor = (-1.0) ** sum(name) / FACTORIAL[spot]
            work[spot * ROWS : (spot + 1) * ROWS, :] = total * factor

    accumulate((0,))
    accumulate((1, 2, 3, 4, 5))
    line[...] = jnp.zeros_like(line)
    for k in range(3):
        both = work[pl.ds(k, TERMS, stride=ROWS), :] + work[pl.ds(k + 4, TERMS, stride=ROWS), :]
        summed = jnp.sum(both.T, axis=0, keepdims=True)
        line[k : k + 1, 0:TERMS] = summed
        line[k + 4 : k + 5, 0:TERMS] = summed
    if copies is None:
        return
    both = line[...]
    for at in range(devices * 4 // ROWS):
        copies[at * ROWS : (at + 1) * ROWS, :] = both


def pick_ghosts(pack, tiles, ghost_ids, ghosts):
    for out_tile in range(ghost_ids.shape[0]):
        wanted = jnp.broadcast_to(ghost_ids[out_tile : out_tile + 1, :], (ROWS, LANES))
        lane, owner = wanted & (LANES - 1), wanted >> 7
        found = jnp.zeros((ROWS, LANES), f32)
        for tile in range(tiles):
            moved = jnp.take_along_axis(
                pack[tile * ROWS : (tile + 1) * ROWS, :], lane, axis=1, mode="promise_in_bounds"
            )
            found = jnp.where(owner == tile, moved, found)
        ghosts[out_tile * ROWS : (out_tile + 1) * ROWS, :] = found


def pick_positions(pack, tiles, ghost_ids, ghosts):
    low = row_ids() < 4
    pairs = ghost_ids.shape[0] // 2
    lanes, owner, found = [], [], []
    for pair in range(pairs):
        wanted = jnp.where(low, spread(ghost_ids, 2 * pair), spread(ghost_ids, 2 * pair + 1))
        lanes.append(wanted & (LANES - 1))
        owner.append(wanted >> 7)
        found.append(jnp.zeros((ROWS, LANES), f32))
    for tile in range(tiles):
        value = pack[tile * ROWS : (tile + 1) * ROWS, :]
        value = jnp.where(low, value, pltpu.roll(value, 4, 0))
        for pair in range(pairs):
            moved = jnp.take_along_axis(value, lanes[pair], axis=1, mode="promise_in_bounds")
            found[pair] = jnp.where(owner[pair] == tile, moved, found[pair])
    for pair in range(pairs):
        ghosts[pair * ROWS : (pair + 1) * ROWS, :] = found[pair]


def prologue_kernel(
    tiles, devices, deep, offsets_in, strength_in, ids_in, pack, ghosts, leaf,
    offsets, strength, ghost_ids, arrivals, copies, leaving, work, line,
):
    loads = [
        pltpu.make_async_copy(source, target, arrivals.at[number])
        for number, (source, target) in enumerate(
            ((offsets_in, offsets), (strength_in, strength), (ids_in, ghost_ids))
        )
    ]
    for load in loads:
        load.start()
    side_z = 1.0 / deep
    axis = lax.broadcasted_iota(jnp.int32, (3, LANES), 0)
    corner = jnp.where(
        axis == 0,
        lax.axis_index("gx").astype(f32),
        jnp.where(
            axis == 1, lax.axis_index("gy").astype(f32), lax.axis_index("gz").astype(f32) * side_z
        ),
    )
    sides = jnp.where(axis == 2, side_z, 1.0)
    blank = jnp.zeros((1, LANES), f32)
    for load in loads:
        load.wait()
    for tile in range(tiles):
        span = slice(tile * LANES, (tile + 1) * LANES)
        base = tile * ROWS
        pack[base : base + 3, :] = corner + offsets[:, span] * sides
        pack[base + 3 : base + 4, :] = blank
        pack[base + 4 : base + 7, :] = strength[:, span]
        pack[base + 7 : base + 8, :] = blank
    leaf_moments(pack, tiles, devices, copies, work, line)
    store = pltpu.make_async_copy(copies, leaf, leaving.at[0])
    store.start()
    pick_ghosts(pack, tiles, ghost_ids, ghosts)
    store.wait()


def fill_derivatives(gap_x, gap_y, known, deep, table, first, stride):
    far = (jnp.maximum(jnp.abs(gap_x), jnp.abs(gap_y)) >= 3) & known
    weight = jnp.where(far, 1.0, 0.0)
    middle_z = slab_middle(deep)[2]
    r = (gap_x.astype(f32), gap_y.astype(f32), jnp.full((ROWS, LANES), middle_z - 0.5, f32))
    square = r[0] * r[0] + r[1] * r[1] + r[2] * r[2] + core_sq
    inverse = 1.0 / square
    taylor = {(0, 0, 0): lax.rsqrt(square)}
    for spot, triple in enumerate(POWERS):
        degree = sum(triple)
        if degree > 0:
            once, twice = None, None
            for axis in range(3):
                down = list(triple)
                down[axis] -= 1
                if down[axis] >= 0:
                    term = r[axis] * taylor[tuple(down)]
                    once = term if once is None else once + term
                down[axis] -= 1
                if down[axis] >= 0:
                    term = taylor[tuple(down)]
                    twice = term if twice is None else twice + term
            total = once * (-(2.0 * degree - 1.0) / degree)
            if twice is not None:
                total = total - twice * ((degree - 1.0) / degree)
            taylor[triple] = total * inverse
        scaled = taylor[triple] * weight * FACTORIAL[spot]
        table[first + spot * stride : first + spot * stride + 1, :] = scaled[0:1, :]


def quotient(value, by, most):
    whole = jnp.zeros(value.shape, jnp.int32)
    for step in range(1, most):
        whole = whole + (value >= step * by).astype(jnp.int32)
    return whole


def derivative_kernel(wide, tall, deep, table, pair_table):
    columns = wide * tall
    lane = lax.broadcasted_iota(jnp.int32, (ROWS, LANES), 1)
    column_x = quotient(lane, tall, wide)
    column_y = lane - column_x * tall
    gap_x = lax.axis_index("gx") - column_x
    gap_y = lax.axis_index("gy") - column_y
    fill_derivatives(gap_x, gap_y, lane < columns, deep, table, 0, 1)
    share = LANES // columns
    local = quotient(lane, columns, share)
    column = lane - local * columns
    column_x = quotient(column, tall, wide)
    column_y = column - column_x * tall
    groups = columns // share
    for group in range(groups):
        domain = local + group * share
        domain_x = quotient(domain, tall, wide)
        domain_y = domain - domain_x * tall
        fill_derivatives(
            domain_x - column_x, domain_y - column_y, domain < columns, deep, pair_table, group, groups
        )


def split_three(value):
    first = value.astype(bf16).astype(f32)
    rest = value - first
    second = rest.astype(bf16).astype(f32)
    return first, second, rest - second


def join(upper, lower):
    return jnp.where(row_ids() < 4, upper, pltpu.roll(lower, 4, 0))


def store_features(place, ref, parts):
    ref[pl.ds(pl.multiple_of(place * FEATURES, FEATURES), FEATURES), :] = jnp.concatenate(
        parts, axis=0
    ).astype(bf16)


def squares_in_row_three(value):
    square = value * value
    return pltpu.roll(square, 1, 0) + pltpu.roll(square, 2, 0) + pltpu.roll(square, 3, 0)


def centred(tile, middle):
    row = row_ids()
    shift = jnp.where(row == 0, middle[0], jnp.where(row == 1, middle[1], middle[2]))
    return jnp.where(row < 3, tile - shift, 0.0)


def source_features(tile, middle, place, sources, pushes):
    row = row_ids()
    here = centred(tile, middle)
    here = jnp.where(row == 3, squares_in_row_three(here) + core_sq, here)
    one, two, three = split_three(here)
    ones = jnp.where(row < 3, 1.0, 0.0)
    store_features(place, sources, [join(one, one), join(two, two), join(one, three), ones])
    push = jnp.where(row >= 4, tile, 0.0)
    one, two, three = split_three(push)
    lines = jnp.concatenate([pltpu.roll(one, 4, 0) + two, pltpu.roll(three, 4, 0)], axis=0).astype(bf16)
    spot = pl.ds(pl.multiple_of(place * 2 * ROWS, 2 * ROWS), 2 * ROWS)
    pushes[spot, 0:LANES] = lines
    pushes[spot, LANES : 2 * LANES] = lines


def target_features(tile, middle, place, targets):
    row = row_ids()
    here = centred(tile, middle)
    size = squares_in_row_three(here)
    one, two, three = split_three(jnp.where(row == 3, 1.0, here * -2.0))
    first, second, third = split_three(size)
    sizes = jnp.where(
        row == 0,
        pltpu.roll(first, 5, 0),
        jnp.where(row == 1, pltpu.roll(second, 6, 0), pltpu.roll(third, 7, 0)),
    )
    sizes = jnp.where(row < 3, sizes, 0.0)
    store_features(place, targets, [join(one, two), join(one, two), join(three, one), sizes])


def block_placer(owners, group, capacity):
    blocks = owners.shape[1]
    own = owners[...].astype(f32)
    down = lax.broadcasted_iota(jnp.int32, (blocks, blocks), 0)
    along = lax.broadcasted_iota(jnp.int32, (blocks, blocks), 1)
    wide = jnp.broadcast_to(own, (blocks, blocks))
    tall = jnp.sum(jnp.where(down == along, wide, 0.0), axis=1, keepdims=True)
    earlier = jnp.where((wide == tall) & (down < along), 1.0, 0.0)
    slot = own * float(capacity) + jnp.sum(earlier, axis=0, keepdims=True)
    place = lax.broadcasted_iota(jnp.int32, (group * capacity, blocks), 0).astype(f32)
    return jnp.where(place == slot, 1.0, 0.0).astype(bf16)


def near_kernel(
    tiles, ghost_tiles, deep, beside, targets_in, sources_in, pack, *rest
):
    count = 2 * len(beside)
    ghost_in, strength_in, rest = rest[:count], rest[count : 2 * count], rest[2 * count :]
    halved = ghost_in[0].shape[0] < strength_in[0].shape[0]
    close, sources, targets, pushes, near, pair_targets, pair_sources, arrivals = rest
    loads = [
        pltpu.make_async_copy(source, target, arrivals.at[number])
        for number, (source, target) in enumerate(
            ((targets_in, pair_targets), (sources_in, pair_sources))
        )
    ]
    for load in loads:
        load.start()
    row = row_ids()
    middle = slab_middle(deep)

    def own_tile(tile, carry):
        value = tile_of(pack, tile)
        source_features(value, middle, tile, sources, pushes)
        target_features(value, middle, tile, targets)
        return carry

    lax.fori_loop(0, tiles, own_tile, 0, unroll=2)
    for number, (name, count) in enumerate(beside):
        index = lax.axis_index(name)
        odd = lax.rem(index, 2) == 1
        has_lower, has_upper = index > 0, index < count - 1

        def ghost_pair(pair, carry, number=number, odd=odd, lows=has_lower, ups=has_upper):
            for which, present in enumerate((lows, ups)):
                def held(refs, tile):
                    one, other = tile_of(refs[2 * number], tile), tile_of(refs[2 * number + 1], tile)
                    return jnp.where(odd, other, one) if which else jnp.where(odd, one, other)

                base = tiles + (2 * number + which) * ghost_tiles
                if halved:
                    both = held(ghost_in, pair)
                for half in range(2):
                    tile = 2 * pair + half
                    value = held(strength_in, tile)
                    if halved:
                        value = jnp.where(row < 4, pltpu.roll(both, 4, 0) if half else both, value)
                    value = jnp.where((row < 4) | present, value, 0.0)
                    source_features(value, middle, base + tile, sources, pushes)
            return carry

        lax.fori_loop(0, ghost_tiles // 2, ghost_pair, 0)

    near[...] = jnp.zeros_like(near)
    for load in loads:
        load.wait()
    pair_count = pair_targets.shape[0]
    batch = BATCH if pair_count % BATCH == 0 else 1

    def batch_of_pairs(number, carry):
        names = [(pair_targets[number * batch + at], pair_sources[number * batch + at]) for at in range(batch)]

        def gap_of(at):
            here, there = names[at]
            return lax.dot_general(
                sources[pl.ds(pl.multiple_of(there * FEATURES, FEATURES), FEATURES), :],
                targets[pl.ds(pl.multiple_of(here * FEATURES, FEATURES), FEATURES), :],
                (((0,), (0,)), ((), ())),
                preferred_element_type=f32,
            )

        def gain_of(at, gap):
            there = names[at][1]
            kernel_block = lax.rsqrt(jnp.maximum(gap, core_sq))
            coarse = kernel_block.astype(bf16)
            fine = (kernel_block - coarse.astype(f32)).astype(bf16)
            return jnp.dot(
                pushes[pl.ds(pl.multiple_of(there * 2 * ROWS, 2 * ROWS), 2 * ROWS), :],
                jnp.concatenate([coarse, fine], axis=0),
                preferred_element_type=f32,
            )

        def add(at, gain):
            spot = pl.ds(pl.multiple_of(names[at][0] * 2 * ROWS, 2 * ROWS), 2 * ROWS)
            near[spot, :] = near[spot, :] + gain

        gaps, gains = {}, {}
        for at in range(batch + LEAD + LAG):
            if at < batch:
                gaps[at] = gap_of(at)
            if 0 <= at - LEAD < batch:
                gains[at - LEAD] = gain_of(at - LEAD, gaps.pop(at - LEAD))
            if 0 <= at - LEAD - LAG < batch:
                add(at - LEAD - LAG, gains.pop(at - LEAD - LAG))
        return carry

    lax.fori_loop(0, pair_count // batch, batch_of_pairs, 0)

    def collect(tile, carry):
        spot = pl.multiple_of(tile * 2 * ROWS, 2 * ROWS)
        upper, lower = near[pl.ds(spot, ROWS), :], near[pl.ds(spot + ROWS, ROWS), :]
        close[pl.ds(pl.multiple_of(tile * ROWS, ROWS), ROWS), :] = upper + pltpu.roll(upper, 4, 0) + lower
        return carry

    lax.fori_loop(0, tiles, collect, 0, unroll=4)


def local_field(place, expansion, base):
    x, y, z = place
    over_x = None
    for a in range(ORDER, -1, -1):
        over_y = None
        for b in range(ORDER - a, -1, -1):
            over_z = None
            for c in range(ORDER - a - b, -1, -1):
                spot = base + PLACE[a, b, c] * ROWS
                factor = expansion[spot : spot + ROWS, :]
                over_z = factor if over_z is None else over_z * z + factor
            over_y = over_z if over_y is None else over_y * y + over_z
        over_x = over_y if over_x is None else over_x * x + over_y
    return over_x


def far_kernel(
    tiles, wide, tall, deep, ghost_ids, pack, close, received, table,
    pack_out, ghosts, speed, work, expansion, square,
):
    columns = wide * tall
    row = row_ids()
    middle = slab_middle(deep)

    square[...] = jnp.zeros_like(square)
    work[...] = jnp.zeros_like(work)
    for k in range(3):
        total = received[pl.ds(k, columns, stride=4 * deep), :]
        for slab in range(1, deep):
            total = total + received[pl.ds(slab * 4 + k, columns, stride=4 * deep), :]
        square[0:columns, :] = total
        turned = square[...].T[0:TERMS, :]
        work[pl.ds(k, TERMS, stride=ROWS), :] = turned
        work[pl.ds(k + 4, TERMS, stride=ROWS), :] = turned
    for spot, outer in enumerate(POWERS):
        total = None
        for inner_spot, inner in enumerate(POWERS):
            if sum(outer) + sum(inner) > ORDER:
                continue
            merged = tuple(o + i for o, i in zip(outer, inner))
            term = spread(table, PLACE[merged]) * work[inner_spot * ROWS : (inner_spot + 1) * ROWS, :]
            total = term if total is None else total + term
        summed = jnp.sum(total, axis=1, keepdims=True) * (1.0 / FACTORIAL[spot])
        expansion[spot * ROWS : (spot + 1) * ROWS, :] = jnp.broadcast_to(summed, (ROWS, LANES))

    def evaluate(pair, carry):
        total = local_field(relative_pair(pack, pair, middle), expansion, 0)
        spot = pl.multiple_of(pair * (2 * ROWS), 2 * ROWS)
        speed[pl.ds(spot, ROWS), :] = total
        speed[pl.ds(spot + ROWS, ROWS), :] = pltpu.roll(total, 4, 0)
        return carry

    lax.fori_loop(0, tiles // 2, evaluate, 0, unroll=4)

    def advance(tile, carry):
        place = pl.ds(pl.multiple_of(tile * ROWS, ROWS), ROWS)
        velocity = jnp.where(row < 3, close[place, :] + speed[place, :], 0.0)
        later = pack[place, :] + time_step * velocity
        pack_out[place, :] = later
        return carry

    lax.fori_loop(0, tiles, advance, 0, unroll=4)
    pick_positions(pack_out, tiles, ghost_ids, ghosts)


def moments_kernel(tiles, pack, line, work):
    leaf_moments(pack, tiles, 0, None, work, line)


def handover_kernel(tiles, group, capacity, owners_in, pack, close, line, sent, owners, arrival):
    load = pltpu.make_async_copy(owners_in, owners, arrival.at[0])
    load.start()
    load.wait()
    placer = block_placer(owners, group, capacity)
    size = 6 * capacity + 4
    slot = lax.broadcasted_iota(jnp.int32, (group * capacity, LANES), 0)
    lane = lax.broadcasted_iota(jnp.int32, (group * capacity, LANES), 1)
    filled = jnp.sum(placer.astype(f32), axis=1, keepdims=True)
    filled = jnp.where(lane == lax.rem(slot, capacity), filled, 0.0)
    placer = jnp.concatenate([placer] * 3, axis=1)
    row = row_ids()
    column = jnp.where(row < 3, line[...], 0.0)[0:4, :]
    for owner in range(group):
        base = owner * size + 6 * capacity
        sent[base : base + 3, :] = column[0:3, :]
        slots = filled[owner * capacity : (owner + 1) * capacity, :]
        sent[base + 3 : base + 4, :] = jnp.sum(slots, axis=0, keepdims=True)
    for field in range(6):
        values = (pack if field < 3 else close)[pl.ds(field % 3, tiles, stride=ROWS), :]
        values = jnp.concatenate([value.astype(bf16) for value in split_three(values)], axis=0)
        placed = jnp.dot(placer, values, preferred_element_type=f32)
        for owner in range(group):
            base = owner * size + field * capacity
            sent[base : base + capacity, :] = placed[owner * capacity : (owner + 1) * capacity, :]


def finish_kernel(wide, tall, deep, capacity, handed, table, positions, velocity, work, sums, expansion, square):
    columns = wide * tall
    size = 6 * capacity + 4
    share = LANES // columns
    groups = columns // share
    row = row_ids()
    lane = lax.broadcasted_iota(jnp.int32, (ROWS, LANES), 1)
    low = row < 4
    part = jnp.where(low, row, row - 4)
    work[...] = jnp.zeros_like(work)
    for k in range(3):
        total = handed[pl.ds(6 * capacity + k, columns, stride=size), :]
        for copy in range(share):
            square[copy * columns : (copy + 1) * columns, :] = total
        turned = square[...].T[0:TERMS, :]
        work[pl.ds(k, TERMS, stride=ROWS), :] = turned
        work[pl.ds(k + 4, TERMS, stride=ROWS), :] = turned

    def expand(group, carry):
        for spot, outer in enumerate(POWERS):
            total = None
            for inner_spot, inner in enumerate(POWERS):
                if sum(outer) + sum(inner) > ORDER:
                    continue
                merged = tuple(o + i for o, i in zip(outer, inner))
                factor = spread(table, PLACE[merged] * groups + group)
                term = factor * work[inner_spot * ROWS : (inner_spot + 1) * ROWS, :]
                total = term if total is None else total + term
            step = columns // 2
            while step:
                total = total + pltpu.roll(total, LANES - step, 1)
                step //= 2
            at = (group * TERMS + spot) * ROWS
            sums[pl.ds(pl.multiple_of(at, ROWS), ROWS), :] = total * (1.0 / FACTORIAL[spot])
        return carry

    lax.fori_loop(0, groups, expand, 0)
    reached = [
        sender
        for sender in range(columns)
        if max(sender // tall, wide - 1 - sender // tall, sender % tall, tall - 1 - sender % tall) >= 3
    ]
    for sender in reached:
        group, local = divmod(sender, share)
        for spot in range(TERMS):
            at = (sender * TERMS + spot) * ROWS
            value = sums[(group * TERMS + spot) * ROWS : (group * TERMS + spot + 1) * ROWS, :]
            expansion[at : at + ROWS, :] = jnp.broadcast_to(
                value[:, local * columns : local * columns + 1], (ROWS, LANES)
            )
    middle_z = slab_middle(deep)[2]
    for sender in range(columns):
        middle = (sender // tall + 0.5, sender % tall + 0.5, middle_z)
        base = sender * size
        flags = spread(handed, base + 6 * capacity + 3)
        for first in range(0, capacity, 2):
            fields = [
                jnp.where(
                    low,
                    spread(handed, base + field * capacity + first),
                    spread(handed, base + field * capacity + first + 1),
                )
                for field in range(6)
            ]
            here = jnp.where(part == 0, fields[0], jnp.where(part == 1, fields[1], fields[2]))
            close = jnp.where(part == 0, fields[3], jnp.where(part == 1, fields[4], fields[5]))
            place = [fields[axis] - middle[axis] for axis in range(3)]
            speed = close
            if sender in reached:
                speed = speed + local_field(place, expansion, sender * TERMS * ROWS)
            picked = jnp.where(lane == jnp.where(low, first, first + 1), flags, 0.0)
            there = jnp.sum(picked, axis=1, keepdims=True) > 0.5
            speed = jnp.where(there, speed, 0.0)
            later = jnp.where(there, here + time_step * speed, 0.0)
            for half in range(2):
                slot = sender * capacity + first + half
                for axis in range(3):
                    at = 4 * half + axis
                    positions[axis, slot : slot + 1, :] = later[at : at + 1, :]
                    velocity[axis, slot : slot + 1, :] = speed[at : at + 1, :]


def even_pairs(block, name):
    count = lax.axis_size(name)
    if count == 1:
        return block
    return lax.ppermute(block, name, [(i, i ^ 1) for i in range(count)])


def odd_pairs(block, name):
    count, deep = lax.axis_size(name), lax.axis_size("gz")
    if count <= 2:
        return block
    if name == "gz" or deep % 2:
        return lax.ppermute(
            block, name, [(i, (i + 1) % count if i % 2 else (i - 1) % count) for i in range(count)]
        )
    moves = []
    for i in range(count):
        for k in range(deep):
            end = i in (0, count - 1)
            other = i * deep + (k ^ 1) if end else (i + 1 if i % 2 else i - 1) * deep + k
            moves.append((i * deep + k, other))
    return lax.ppermute(block, (name, "gz"), moves)


def per_device(offsets, strength, ghost_list, pair_targets, pair_sources, owners):
    wide, tall, deep = (lax.axis_size(name) for name in everywhere)
    devices, group = wide * tall * deep, wide * tall
    segments = offsets.shape[1]
    tiles = segments // LANES
    ghost_tiles = ghost_list.shape[0] // LANES
    capacity = max(2, 2 * tiles // group)
    ghost_ids = ghost_list.reshape(ghost_tiles, LANES)
    in_vmem = pl.BlockSpec(memory_space=pltpu.VMEM)
    pack_type = jax.ShapeDtypeStruct((tiles * ROWS, LANES), f32)
    leaf_type = jax.ShapeDtypeStruct((devices * 4, LANES), f32)
    ghost_type = jax.ShapeDtypeStruct((ghost_tiles * ROWS, LANES), f32)
    work = pltpu.VMEM((TERMS * ROWS, LANES), f32)
    line = pltpu.VMEM((ROWS, LANES), f32)
    params = pltpu.CompilerParams(vmem_limit_bytes=48 << 20)

    in_place = pl.BlockSpec(memory_space=pltpu.HBM)
    in_hbm = functools.partial(pltpu.with_memory_space_constraint, memory_space=pltpu.HBM)

    copies = pltpu.VMEM((devices * 4, LANES), f32)
    square = pltpu.VMEM((LANES, LANES), f32)
    gather_moments = pl.pallas_call(
        functools.partial(moments_kernel, tiles),
        out_shape=jax.ShapeDtypeStruct((ROWS, LANES), f32),
        in_specs=[in_vmem],
        out_specs=in_vmem,
        scratch_shapes=[work],
        compiler_params=params,
        name="moments",
    )
    one_copy = pltpu.SemaphoreType.DMA((1,))

    pack, ghosts, leaf = pl.pallas_call(
        functools.partial(prologue_kernel, tiles, devices, deep),
        out_shape=(pack_type, ghost_type, leaf_type),
        in_specs=[in_place] * 3,
        out_specs=(in_vmem, in_vmem, in_place),
        scratch_shapes=[
            pltpu.VMEM(offsets.shape, f32),
            pltpu.VMEM(strength.shape, f32),
            pltpu.VMEM(ghost_ids.shape, jnp.int32),
            pltpu.SemaphoreType.DMA((3,)),
            copies,
            one_copy,
            work,
            line,
        ],
        compiler_params=params,
        name="prologue",
    )(in_hbm(offsets), in_hbm(strength), in_hbm(ghost_ids))
    table, pair_table = pl.pallas_call(
        functools.partial(derivative_kernel, wide, tall, deep),
        out_shape=(
            jax.ShapeDtypeStruct((TERMS, LANES), f32),
            jax.ShapeDtypeStruct((TERMS * (group * group // LANES), LANES), f32),
        ),
        out_specs=(in_vmem,) * 2,
        compiler_params=params,
        name="derivatives",
    )()
    beside = tuple((name, lax.axis_size(name)) for name in everywhere)
    places = tiles + 2 * len(beside) * ghost_tiles
    for step_number in range(2):
        final = step_number == 1
        arrived = []
        for name, _ in beside:
            arrived.extend((even_pairs(ghosts, name), odd_pairs(ghosts, name)))
        if not final:
            strengths = arrived
        if final:
            slab = gather_moments(pack)
            column = slab + even_pairs(slab, "gz") if deep == 2 else lax.psum(slab, "gz")
        else:
            received = lax.all_to_all(leaf, everywhere, split_axis=0, concat_axis=0, tiled=True)
        close = pl.pallas_call(
            functools.partial(near_kernel, tiles, ghost_tiles, deep, beside),
            out_shape=pack_type,
            in_specs=[in_place] * 2 + [in_vmem] * (1 + 2 * len(arrived)),
            out_specs=in_vmem,
            scratch_shapes=[
                pltpu.VMEM((places * FEATURES, LANES), bf16),
                pltpu.VMEM((tiles * FEATURES, LANES), bf16),
                pltpu.VMEM((places * 2 * ROWS, 2 * LANES), bf16),
                pltpu.VMEM((tiles * 2 * ROWS, LANES), f32),
                pltpu.SMEM(pair_targets.shape, jnp.int32),
                pltpu.SMEM(pair_sources.shape, jnp.int32),
                pltpu.SemaphoreType.DMA((2,)),
            ],
            compiler_params=params,
            name="near",
        )(in_hbm(pair_targets), in_hbm(pair_sources), pack, *arrived, *strengths)
        if not final:
            half_type = jax.ShapeDtypeStruct((ghost_tiles * 4, LANES), f32)
            pack, ghosts = pl.pallas_call(
                functools.partial(far_kernel, tiles, wide, tall, deep),
                out_shape=(pack_type, half_type),
                in_specs=[in_vmem] * 5,
                out_specs=(in_vmem,) * 2,
                scratch_shapes=[pltpu.VMEM((tiles * ROWS, LANES), f32), work, work, square],
                compiler_params=params,
                name="far",
            )(ghost_ids, pack, close, received, table)
    size = 6 * capacity + 4
    sent = pl.pallas_call(
        functools.partial(handover_kernel, tiles, group, capacity),
        out_shape=jax.ShapeDtypeStruct((group * size, LANES), f32),
        in_specs=[in_place] + [in_vmem] * 3,
        out_specs=in_vmem,
        scratch_shapes=[pltpu.VMEM((1, tiles), jnp.int32), one_copy],
        compiler_params=params,
        name="handover",
    )(in_hbm(owners.reshape(1, tiles)), pack, close, column)
    handed = lax.all_to_all(sent, ("gx", "gy"), split_axis=0, concat_axis=0, tiled=True)
    moved = jax.ShapeDtypeStruct((3, group * capacity, LANES), f32)
    moved = pl.pallas_call(
        functools.partial(finish_kernel, wide, tall, deep, capacity),
        out_shape=(moved, moved),
        in_specs=[in_vmem] * 2,
        out_specs=(in_vmem,) * 2,
        scratch_shapes=[
            work,
            pltpu.VMEM((group * group // LANES * TERMS * ROWS, LANES), f32),
            pltpu.VMEM((group * TERMS * ROWS, LANES), f32),
            square,
        ],
        compiler_params=params,
        name="finish",
    )(handed, pair_table)
    return tuple(value.transpose(1, 0, 2) for value in moved)


def solution(mesh):
    return jax.shard_map(
        per_device,
        mesh=mesh,
        in_specs=(
            P(None, everywhere),
            P(None, everywhere),
            P(everywhere),
            P(everywhere),
            P(everywhere),
            P(everywhere, None),
        ),
        out_specs=(P(everywhere, None, None), P(everywhere, None, None)),
        check_vma=False,
    )
```

```python
import functools
import math

import jax
import jax.numpy as jnp
import numpy as np
from jax import lax
from jax.experimental import pallas as pl
from jax.experimental.pallas import tpu as pltpu
from jax.sharding import PartitionSpec as P


ORDER = 5
LANES = 128
ROWS = 8
FEATURES = 32
BATCH = 128
LEAD = 12
LAG = 8

core_sq = 0.0025
time_step = 0.1
everywhere = ("gx", "gy", "gz")
f32 = jnp.float32
bf16 = jnp.bfloat16


def exponents():
    entries = []
    for degree in range(ORDER + 1):
        for leading in range(degree, -1, -1):
            for middle in range(degree - leading, -1, -1):
                entries.append((leading, middle, degree - leading - middle))
    return entries


POWERS = exponents()
TERMS = len(POWERS)
PLACE = {triple: spot for spot, triple in enumerate(POWERS)}
FACTORIAL = [float(np.prod([math.factorial(e) for e in triple])) for triple in POWERS]


def row_ids():
    return lax.broadcasted_iota(jnp.int32, (ROWS, LANES), 0)


def spread(ref, row):
    return ref[pl.ds(row, ROWS, stride=0), :]


def tile_of(ref, tile):
    return ref[pl.ds(pl.multiple_of(tile * ROWS, ROWS), ROWS), :]


def slab_middle(deep):
    side_z = 1.0 / deep
    middle_x = lax.axis_index("gx").astype(f32) + 0.5
    middle_y = lax.axis_index("gy").astype(f32) + 0.5
    middle_z = lax.axis_index("gz").astype(f32) * side_z + 0.5 * side_z
    return middle_x, middle_y, middle_z


def relative_pair(pack, pair, middle):
    low = row_ids() < 4
    base = pair * (2 * ROWS)
    return [
        jnp.where(low, spread(pack, base + axis), spread(pack, base + ROWS + axis)) - middle[axis]
        for axis in range(3)
    ]


def leaf_moments(pack, tiles, devices, copies, work, line):
    middle_x, middle_y, _ = slab_middle(1)
    middle = (middle_x, middle_y, 0.5)
    low = row_ids() < 4

    def accumulate(chosen):
        def body(pair, sums):
            x, y, z = relative_pair(pack, pair, middle)
            even, odd = tile_of(pack, 2 * pair), tile_of(pack, 2 * pair + 1)
            first = jnp.where(low, pltpu.roll(even, 4, 0), odd)
            value = {(0, 0, 0): first}
            gained = []
            for a in range(ORDER + 1):
                if a > 0:
                    value[a, 0, 0] = value[a - 1, 0, 0] * x
                if a not in chosen:
                    continue
                for b in range(ORDER + 1 - a):
                    if b > 0:
                        value[a, b, 0] = value[a, b - 1, 0] * y
                    for c in range(ORDER + 1 - a - b):
                        if c > 0:
                            value[a, b, c] = value[a, b, c - 1] * z
                        gained.append(value[a, b, c])
            return tuple(total + more for total, more in zip(sums, gained))

        names = [
            (a, b, c)
            for a in chosen
            for b in range(ORDER + 1 - a)
            for c in range(ORDER + 1 - a - b)
        ]
        zero = jnp.zeros((ROWS, LANES), f32)
        sums = lax.fori_loop(0, tiles // 2, body, tuple(zero for _ in names), unroll=4)
        for name, total in zip(names, sums):
            spot = PLACE[name]
            factor = (-1.0) ** sum(name) / FACTORIAL[spot]
            work[spot * ROWS : (spot + 1) * ROWS, :] = total * factor

    accumulate((0,))
    accumulate((1, 2, 3, 4, 5))
    line[...] = jnp.zeros_like(line)
    for k in range(3):
        both = work[pl.ds(k, TERMS, stride=ROWS), :] + work[pl.ds(k + 4, TERMS, stride=ROWS), :]
        summed = jnp.sum(both.T, axis=0, keepdims=True)
        line[k : k + 1, 0:TERMS] = summed
        line[k + 4 : k + 5, 0:TERMS] = summed
    if copies is None:
        return
    both = line[...]
    for at in range(devices * 4 // ROWS):
        copies[at * ROWS : (at + 1) * ROWS, :] = both


def pick_ghosts(pack, tiles, ghost_ids, ghosts):
    for out_tile in range(ghost_ids.shape[0]):
        wanted = jnp.broadcast_to(ghost_ids[out_tile : out_tile + 1, :], (ROWS, LANES))
        lane, owner = wanted & (LANES - 1), wanted >> 7
        found = jnp.zeros((ROWS, LANES), f32)
        for tile in range(tiles):
            moved = jnp.take_along_axis(
                pack[tile * ROWS : (tile + 1) * ROWS, :], lane, axis=1, mode="promise_in_bounds"
            )
            found = jnp.where(owner == tile, moved, found)
        ghosts[out_tile * ROWS : (out_tile + 1) * ROWS, :] = found


def pick_positions(pack, tiles, ghost_ids, ghosts):
    low = row_ids() < 4
    pairs = ghost_ids.shape[0] // 2
    lanes, owner, found = [], [], []
    for pair in range(pairs):
        wanted = jnp.where(low, spread(ghost_ids, 2 * pair), spread(ghost_ids, 2 * pair + 1))
        lanes.append(wanted & (LANES - 1))
        owner.append(wanted >> 7)
        found.append(jnp.zeros((ROWS, LANES), f32))
    for tile in range(tiles):
        value = pack[tile * ROWS : (tile + 1) * ROWS, :]
        value = jnp.where(low, value, pltpu.roll(value, 4, 0))
        for pair in range(pairs):
            moved = jnp.take_along_axis(value, lanes[pair], axis=1, mode="promise_in_bounds")
            found[pair] = jnp.where(owner[pair] == tile, moved, found[pair])
    for pair in range(pairs):
        ghosts[pair * ROWS : (pair + 1) * ROWS, :] = found[pair]


def prologue_kernel(
    tiles, devices, deep, offsets_in, strength_in, ids_in, pack, ghosts, leaf,
    offsets, strength, ghost_ids, arrivals, copies, leaving, work, line,
):
    loads = [
        pltpu.make_async_copy(source, target, arrivals.at[number])
        for number, (source, target) in enumerate(
            ((offsets_in, offsets), (strength_in, strength), (ids_in, ghost_ids))
        )
    ]
    for load in loads:
        load.start()
    side_z = 1.0 / deep
    axis = lax.broadcasted_iota(jnp.int32, (3, LANES), 0)
    corner = jnp.where(
        axis == 0,
        lax.axis_index("gx").astype(f32),
        jnp.where(
            axis == 1, lax.axis_index("gy").astype(f32), lax.axis_index("gz").astype(f32) * side_z
        ),
    )
    sides = jnp.where(axis == 2, side_z, 1.0)
    blank = jnp.zeros((1, LANES), f32)
    for load in loads:
        load.wait()
    for tile in range(tiles):
        span = slice(tile * LANES, (tile + 1) * LANES)
        base = tile * ROWS
        pack[base : base + 3, :] = corner + offsets[:, span] * sides
        pack[base + 3 : base + 4, :] = blank
        pack[base + 4 : base + 7, :] = strength[:, span]
        pack[base + 7 : base + 8, :] = blank
    leaf_moments(pack, tiles, devices, copies, work, line)
    store = pltpu.make_async_copy(copies, leaf, leaving.at[0])
    store.start()
    pick_ghosts(pack, tiles, ghost_ids, ghosts)
    store.wait()


def fill_derivatives(gap_x, gap_y, known, deep, table, first, stride):
    far = (jnp.maximum(jnp.abs(gap_x), jnp.abs(gap_y)) >= 3) & known
    weight = jnp.where(far, 1.0, 0.0)
    middle_z = slab_middle(deep)[2]
    r = (gap_x.astype(f32), gap_y.astype(f32), jnp.full((ROWS, LANES), middle_z - 0.5, f32))
    square = r[0] * r[0] + r[1] * r[1] + r[2] * r[2] + core_sq
    inverse = 1.0 / square
    taylor = {(0, 0, 0): lax.rsqrt(square)}
    for spot, triple in enumerate(POWERS):
        degree = sum(triple)
        if degree > 0:
            once, twice = None, None
            for axis in range(3):
                down = list(triple)
                down[axis] -= 1
                if down[axis] >= 0:
                    term = r[axis] * taylor[tuple(down)]
                    once = term if once is None else once + term
                down[axis] -= 1
                if down[axis] >= 0:
                    term = taylor[tuple(down)]
                    twice = term if twice is None else twice + term
            total = once * (-(2.0 * degree - 1.0) / degree)
            if twice is not None:
                total = total - twice * ((degree - 1.0) / degree)
            taylor[triple] = total * inverse
        scaled = taylor[triple] * weight * FACTORIAL[spot]
        table[first + spot * stride : first + spot * stride + 1, :] = scaled[0:1, :]


def quotient(value, by, most):
    whole = jnp.zeros(value.shape, jnp.int32)
    for step in range(1, most):
        whole = whole + (value >= step * by).astype(jnp.int32)
    return whole


def block_placer(owners, group, capacity):
    blocks = owners.shape[1]
    own = owners[...].astype(f32)
    down = lax.broadcasted_iota(jnp.int32, (blocks, blocks), 0)
    along = lax.broadcasted_iota(jnp.int32, (blocks, blocks), 1)
    wide = jnp.broadcast_to(own, (blocks, blocks))
    tall = jnp.sum(jnp.where(down == along, wide, 0.0), axis=1, keepdims=True)
    earlier = jnp.where((wide == tall) & (down < along), 1.0, 0.0)
    slot = own * float(capacity) + jnp.sum(earlier, axis=0, keepdims=True)
    place = lax.broadcasted_iota(jnp.int32, (group * capacity, blocks), 0).astype(f32)
    return jnp.where(place == slot, 1.0, 0.0).astype(bf16)


def geometry_kernel(wide, tall, deep, capacity, owners_in, table, pair_table, placer_out, flags, owners, arrival):
    load = pltpu.make_async_copy(owners_in, owners, arrival.at[0])
    load.start()
    columns = wide * tall
    lane = lax.broadcasted_iota(jnp.int32, (ROWS, LANES), 1)
    column_x = quotient(lane, tall, wide)
    column_y = lane - column_x * tall
    gap_x = lax.axis_index("gx") - column_x
    gap_y = lax.axis_index("gy") - column_y
    fill_derivatives(gap_x, gap_y, lane < columns, deep, table, 0, 1)
    share = LANES // columns
    local = quotient(lane, columns, share)
    column = lane - local * columns
    column_x = quotient(column, tall, wide)
    column_y = column - column_x * tall
    groups = columns // share
    for group in range(groups):
        domain = local + group * share
        domain_x = quotient(domain, tall, wide)
        domain_y = domain - domain_x * tall
        fill_derivatives(
            domain_x - column_x, domain_y - column_y, domain < columns, deep, pair_table, group, groups
        )
    load.wait()
    placer = block_placer(owners, columns, capacity)
    slot = lax.broadcasted_iota(jnp.int32, (columns * capacity, LANES), 0)
    place = lax.broadcasted_iota(jnp.int32, (columns * capacity, LANES), 1)
    filled = jnp.sum(placer.astype(f32), axis=1, keepdims=True)
    filled = jnp.where(place == lax.rem(slot, capacity), filled, 0.0)
    for owner in range(columns):
        slots = filled[owner * capacity : (owner + 1) * capacity, :]
        flags[owner : owner + 1, :] = jnp.sum(slots, axis=0, keepdims=True)
    placer_out[...] = jnp.concatenate([placer] * 3, axis=1)


def split_three(value):
    first = value.astype(bf16).astype(f32)
    rest = value - first
    second = rest.astype(bf16).astype(f32)
    return first, second, rest - second


def join(upper, lower):
    return jnp.where(row_ids() < 4, upper, pltpu.roll(lower, 4, 0))


def store_features(place, ref, parts):
    ref[pl.ds(pl.multiple_of(place * FEATURES, FEATURES), FEATURES), :] = jnp.concatenate(
        parts, axis=0
    ).astype(bf16)


def squares_in_row_three(value):
    square = value * value
    return pltpu.roll(square, 1, 0) + pltpu.roll(square, 2, 0) + pltpu.roll(square, 3, 0)


def centred(tile, middle):
    row = row_ids()
    shift = jnp.where(row == 0, middle[0], jnp.where(row == 1, middle[1], middle[2]))
    return jnp.where(row < 3, tile - shift, 0.0)


def source_features(tile, middle, place, sources, pushes):
    row = row_ids()
    here = centred(tile, middle)
    here = jnp.where(row == 3, squares_in_row_three(here) + core_sq, here)
    one, two, three = split_three(here)
    ones = jnp.where(row < 3, 1.0, 0.0)
    store_features(place, sources, [join(one, one), join(two, two), join(one, three), ones])
    push = jnp.where(row >= 4, tile, 0.0)
    one, two, three = split_three(push)
    lines = jnp.concatenate([pltpu.roll(one, 4, 0) + two, pltpu.roll(three, 4, 0)], axis=0).astype(bf16)
    spot = pl.ds(pl.multiple_of(place * 2 * ROWS, 2 * ROWS), 2 * ROWS)
    pushes[spot, 0:LANES] = lines
    pushes[spot, LANES : 2 * LANES] = lines


def target_features(tile, middle, place, targets):
    row = row_ids()
    here = centred(tile, middle)
    size = squares_in_row_three(here)
    one, two, three = split_three(jnp.where(row == 3, 1.0, here * -2.0))
    first, second, third = split_three(size)
    sizes = jnp.where(
        row == 0,
        pltpu.roll(first, 5, 0),
        jnp.where(row == 1, pltpu.roll(second, 6, 0), pltpu.roll(third, 7, 0)),
    )
    sizes = jnp.where(row < 3, sizes, 0.0)
    store_features(place, targets, [join(one, two), join(one, two), join(three, one), sizes])


def near_kernel(
    tiles, ghost_tiles, deep, beside, targets_in, sources_in, pack, *rest
):
    count = 2 * len(beside)
    ghost_in, strength_in, rest = rest[:count], rest[count : 2 * count], rest[2 * count :]
    halved = ghost_in[0].shape[0] < strength_in[0].shape[0]
    close, sources, targets, pushes, near, pair_targets, pair_sources, arrivals = rest
    loads = [
        pltpu.make_async_copy(source, target, arrivals.at[number])
        for number, (source, target) in enumerate(
            ((targets_in, pair_targets), (sources_in, pair_sources))
        )
    ]
    for load in loads:
        load.start()
    row = row_ids()
    middle = slab_middle(deep)

    def own_tile(tile, carry):
        value = tile_of(pack, tile)
        source_features(value, middle, tile, sources, pushes)
        target_features(value, middle, tile, targets)
        return carry

    lax.fori_loop(0, tiles, own_tile, 0, unroll=2)
    for number, (name, count) in enumerate(beside):
        index = lax.axis_index(name)
        odd = lax.rem(index, 2) == 1
        has_lower, has_upper = index > 0, index < count - 1

        def ghost_pair(pair, carry, number=number, odd=odd, lows=has_lower, ups=has_upper):
            for which, present in enumerate((lows, ups)):
                def held(refs, tile):
                    one, other = tile_of(refs[2 * number], tile), tile_of(refs[2 * number + 1], tile)
                    return jnp.where(odd, other, one) if which else jnp.where(odd, one, other)

                base = tiles + (2 * number + which) * ghost_tiles
                if halved:
                    both = held(ghost_in, pair)
                for half in range(2):
                    tile = 2 * pair + half
                    value = held(strength_in, tile)
                    if halved:
                        value = jnp.where(row < 4, pltpu.roll(both, 4, 0) if half else both, value)
                    value = jnp.where((row < 4) | present, value, 0.0)
                    source_features(value, middle, base + tile, sources, pushes)
            return carry

        lax.fori_loop(0, ghost_tiles // 2, ghost_pair, 0)

    near[...] = jnp.zeros_like(near)
    for load in loads:
        load.wait()
    pair_count = pair_targets.shape[0]
    batch = BATCH if pair_count % BATCH == 0 else 1

    def batch_of_pairs(number, carry):
        names = [(pair_targets[number * batch + at], pair_sources[number * batch + at]) for at in range(batch)]

        def gap_of(at):
            here, there = names[at]
            return lax.dot_general(
                sources[pl.ds(pl.multiple_of(there * FEATURES, FEATURES), FEATURES), :],
                targets[pl.ds(pl.multiple_of(here * FEATURES, FEATURES), FEATURES), :],
                (((0,), (0,)), ((), ())),
                preferred_element_type=f32,
            )

        def gain_of(at, gap):
            there = names[at][1]
            kernel_block = lax.rsqrt(jnp.maximum(gap, core_sq))
            coarse = kernel_block.astype(bf16)
            fine = (kernel_block - coarse.astype(f32)).astype(bf16)
            return jnp.dot(
                pushes[pl.ds(pl.multiple_of(there * 2 * ROWS, 2 * ROWS), 2 * ROWS), :],
                jnp.concatenate([coarse, fine], axis=0),
                preferred_element_type=f32,
            )

        def add(at, gain):
            spot = pl.ds(pl.multiple_of(names[at][0] * 2 * ROWS, 2 * ROWS), 2 * ROWS)
            near[spot, :] = near[spot, :] + gain

        gaps, gains = {}, {}
        for at in range(batch + LEAD + LAG):
            if at < batch:
                gaps[at] = gap_of(at)
            if 0 <= at - LEAD < batch:
                gains[at - LEAD] = gain_of(at - LEAD, gaps.pop(at - LEAD))
            if 0 <= at - LEAD - LAG < batch:
                add(at - LEAD - LAG, gains.pop(at - LEAD - LAG))
        return carry

    lax.fori_loop(0, pair_count // batch, batch_of_pairs, 0)

    def collect(tile, carry):
        spot = pl.multiple_of(tile * 2 * ROWS, 2 * ROWS)
        upper, lower = near[pl.ds(spot, ROWS), :], near[pl.ds(spot + ROWS, ROWS), :]
        close[pl.ds(pl.multiple_of(tile * ROWS, ROWS), ROWS), :] = upper + pltpu.roll(upper, 4, 0) + lower
        return carry

    lax.fori_loop(0, tiles, collect, 0, unroll=4)


def local_field(place, expansion, base):
    x, y, z = place
    over_x = None
    for a in range(ORDER, -1, -1):
        over_y = None
        for b in range(ORDER - a, -1, -1):
            over_z = None
            for c in range(ORDER - a - b, -1, -1):
                spot = base + PLACE[a, b, c] * ROWS
                factor = expansion[spot : spot + ROWS, :]
                over_z = factor if over_z is None else over_z * z + factor
            over_y = over_z if over_y is None else over_y * y + over_z
        over_x = over_y if over_x is None else over_x * x + over_y
    return over_x


def far_kernel(
    tiles, wide, tall, deep, ghost_ids, pack, close, received, table,
    pack_out, ghosts, speed, work, expansion, square,
):
    columns = wide * tall
    row = row_ids()
    middle = slab_middle(deep)

    square[...] = jnp.zeros_like(square)
    work[...] = jnp.zeros_like(work)
    for k in range(3):
        total = received[pl.ds(k, columns, stride=4 * deep), :]
        for slab in range(1, deep):
            total = total + received[pl.ds(slab * 4 + k, columns, stride=4 * deep), :]
        square[0:columns, :] = total
        turned = square[...].T[0:TERMS, :]
        work[pl.ds(k, TERMS, stride=ROWS), :] = turned
        work[pl.ds(k + 4, TERMS, stride=ROWS), :] = turned
    for spot, outer in enumerate(POWERS):
        total = None
        for inner_spot, inner in enumerate(POWERS):
            if sum(outer) + sum(inner) > ORDER:
                continue
            merged = tuple(o + i for o, i in zip(outer, inner))
            term = spread(table, PLACE[merged]) * work[inner_spot * ROWS : (inner_spot + 1) * ROWS, :]
            total = term if total is None else total + term
        summed = jnp.sum(total, axis=1, keepdims=True) * (1.0 / FACTORIAL[spot])
        expansion[spot * ROWS : (spot + 1) * ROWS, :] = jnp.broadcast_to(summed, (ROWS, LANES))

    def evaluate(pair, carry):
        total = local_field(relative_pair(pack, pair, middle), expansion, 0)
        spot = pl.multiple_of(pair * (2 * ROWS), 2 * ROWS)
        speed[pl.ds(spot, ROWS), :] = total
        speed[pl.ds(spot + ROWS, ROWS), :] = pltpu.roll(total, 4, 0)
        return carry

    lax.fori_loop(0, tiles // 2, evaluate, 0, unroll=4)

    def advance(tile, carry):
        place = pl.ds(pl.multiple_of(tile * ROWS, ROWS), ROWS)
        velocity = jnp.where(row < 3, close[place, :] + speed[place, :], 0.0)
        later = pack[place, :] + time_step * velocity
        pack_out[place, :] = later
        return carry

    lax.fori_loop(0, tiles, advance, 0, unroll=4)
    pick_positions(pack_out, tiles, ghost_ids, ghosts)


def moments_kernel(tiles, pack, line, work):
    leaf_moments(pack, tiles, 0, None, work, line)


def handover_kernel(tiles, group, capacity, placer, flags, pack, close, *rest):
    slabs, sent = rest[:-1], rest[-1]
    size = 6 * capacity + 4
    column = slabs[0][...]
    for slab in slabs[1:]:
        column = column + slab[...]
    for owner in range(group):
        base = owner * size + 6 * capacity
        sent[base : base + 3, :] = column[0:3, :]
        sent[base + 3 : base + 4, :] = flags[owner : owner + 1, :]
    for field in range(6):
        values = (pack if field < 3 else close)[pl.ds(field % 3, tiles, stride=ROWS), :]
        values = jnp.concatenate([value.astype(bf16) for value in split_three(values)], axis=0)
        placed = jnp.dot(placer[...], values, preferred_element_type=f32)
        for owner in range(group):
            base = owner * size + field * capacity
            sent[base : base + capacity, :] = placed[owner * capacity : (owner + 1) * capacity, :]


def finish_kernel(wide, tall, deep, capacity, handed, table, positions, velocity, work, sums, expansion, square):
    columns = wide * tall
    size = 6 * capacity + 4
    share = LANES // columns
    groups = columns // share
    row = row_ids()
    lane = lax.broadcasted_iota(jnp.int32, (ROWS, LANES), 1)
    low = row < 4
    part = jnp.where(low, row, row - 4)
    work[...] = jnp.zeros_like(work)
    for k in range(3):
        total = handed[pl.ds(6 * capacity + k, columns, stride=size), :]
        for copy in range(share):
            square[copy * columns : (copy + 1) * columns, :] = total
        turned = square[...].T[0:TERMS, :]
        work[pl.ds(k, TERMS, stride=ROWS), :] = turned
        work[pl.ds(k + 4, TERMS, stride=ROWS), :] = turned

    def expand(group, carry):
        for spot, outer in enumerate(POWERS):
            total = None
            for inner_spot, inner in enumerate(POWERS):
                if sum(outer) + sum(inner) > ORDER:
                    continue
                merged = tuple(o + i for o, i in zip(outer, inner))
                factor = spread(table, PLACE[merged] * groups + group)
                term = factor * work[inner_spot * ROWS : (inner_spot + 1) * ROWS, :]
                total = term if total is None else total + term
            at = (group * TERMS + spot) * ROWS
            sums[pl.ds(pl.multiple_of(at, ROWS), ROWS), :] = total * (1.0 / FACTORIAL[spot])
        return carry

    lax.fori_loop(0, groups, expand, 0)
    step = columns // 2
    while step:
        sums[...] = sums[...] + pltpu.roll(sums[...], LANES - step, 1)
        step //= 2
    reached = [
        sender
        for sender in range(columns)
        if max(sender // tall, wide - 1 - sender // tall, sender % tall, tall - 1 - sender % tall) >= 3
    ]
    for sender in reached:
        group, local = divmod(sender, share)
        for spot in range(TERMS):
            at = (sender * TERMS + spot) * ROWS
            value = sums[(group * TERMS + spot) * ROWS : (group * TERMS + spot + 1) * ROWS, :]
            expansion[at : at + ROWS, :] = jnp.broadcast_to(
                value[:, local * columns : local * columns + 1], (ROWS, LANES)
            )
    middle_z = slab_middle(deep)[2]
    for sender in range(columns):
        middle = (sender // tall + 0.5, sender % tall + 0.5, middle_z)
        base = sender * size
        flags = spread(handed, base + 6 * capacity + 3)
        for first in range(0, capacity, 2):
            fields = [
                jnp.where(
                    low,
                    spread(handed, base + field * capacity + first),
                    spread(handed, base + field * capacity + first + 1),
                )
                for field in range(6)
            ]
            here = jnp.where(part == 0, fields[0], jnp.where(part == 1, fields[1], fields[2]))
            close = jnp.where(part == 0, fields[3], jnp.where(part == 1, fields[4], fields[5]))
            place = [fields[axis] - middle[axis] for axis in range(3)]
            speed = close
            if sender in reached:
                speed = speed + local_field(place, expansion, sender * TERMS * ROWS)
            picked = jnp.where(lane == jnp.where(low, first, first + 1), flags, 0.0)
            there = jnp.sum(picked, axis=1, keepdims=True) > 0.5
            speed = jnp.where(there, speed, 0.0)
            later = jnp.where(there, here + time_step * speed, 0.0)
            for half in range(2):
                slot = sender * capacity + first + half
                for axis in range(3):
                    at = 4 * half + axis
                    positions[axis, slot : slot + 1, :] = later[at : at + 1, :]
                    velocity[axis, slot : slot + 1, :] = speed[at : at + 1, :]


def even_pairs(block, name):
    count = lax.axis_size(name)
    if count == 1:
        return block
    return lax.ppermute(block, name, [(i, i ^ 1) for i in range(count)])


def odd_pairs(block, name):
    count, deep = lax.axis_size(name), lax.axis_size("gz")
    if count <= 2:
        return block
    if name == "gz" or deep % 2:
        return lax.ppermute(
            block, name, [(i, (i + 1) % count if i % 2 else (i - 1) % count) for i in range(count)]
        )
    moves = []
    for i in range(count):
        for k in range(deep):
            end = i in (0, count - 1)
            other = i * deep + (k ^ 1) if end else (i + 1 if i % 2 else i - 1) * deep + k
            moves.append((i * deep + k, other))
    return lax.ppermute(block, (name, "gz"), moves)


def per_device(offsets, strength, ghost_list, pair_targets, pair_sources, owners):
    wide, tall, deep = (lax.axis_size(name) for name in everywhere)
    devices, group = wide * tall * deep, wide * tall
    segments = offsets.shape[1]
    tiles = segments // LANES
    ghost_tiles = ghost_list.shape[0] // LANES
    capacity = max(2, 2 * tiles // group)
    ghost_ids = ghost_list.reshape(ghost_tiles, LANES)
    in_vmem = pl.BlockSpec(memory_space=pltpu.VMEM)
    pack_type = jax.ShapeDtypeStruct((tiles * ROWS, LANES), f32)
    leaf_type = jax.ShapeDtypeStruct((devices * 4, LANES), f32)
    ghost_type = jax.ShapeDtypeStruct((ghost_tiles * ROWS, LANES), f32)
    work = pltpu.VMEM((TERMS * ROWS, LANES), f32)
    line = pltpu.VMEM((ROWS, LANES), f32)
    params = pltpu.CompilerParams(vmem_limit_bytes=48 << 20)

    in_place = pl.BlockSpec(memory_space=pltpu.HBM)
    in_hbm = functools.partial(pltpu.with_memory_space_constraint, memory_space=pltpu.HBM)

    copies = pltpu.VMEM((devices * 4, LANES), f32)
    square = pltpu.VMEM((LANES, LANES), f32)
    gather_moments = pl.pallas_call(
        functools.partial(moments_kernel, tiles),
        out_shape=jax.ShapeDtypeStruct((ROWS, LANES), f32),
        in_specs=[in_vmem],
        out_specs=in_vmem,
        scratch_shapes=[work],
        compiler_params=params,
        name="moments",
    )
    one_copy = pltpu.SemaphoreType.DMA((1,))

    pack, ghosts, leaf = pl.pallas_call(
        functools.partial(prologue_kernel, tiles, devices, deep),
        out_shape=(pack_type, ghost_type, leaf_type),
        in_specs=[in_place] * 3,
        out_specs=(in_vmem, in_vmem, in_place),
        scratch_shapes=[
            pltpu.VMEM(offsets.shape, f32),
            pltpu.VMEM(strength.shape, f32),
            pltpu.VMEM(ghost_ids.shape, jnp.int32),
            pltpu.SemaphoreType.DMA((3,)),
            copies,
            one_copy,
            work,
            line,
        ],
        compiler_params=params,
        name="prologue",
    )(in_hbm(offsets), in_hbm(strength), in_hbm(ghost_ids))
    table, pair_table, placer, flags = pl.pallas_call(
        functools.partial(geometry_kernel, wide, tall, deep, capacity),
        out_shape=(
            jax.ShapeDtypeStruct((TERMS, LANES), f32),
            jax.ShapeDtypeStruct((TERMS * (group * group // LANES), LANES), f32),
            jax.ShapeDtypeStruct((group * capacity, 3 * tiles), bf16),
            jax.ShapeDtypeStruct((group, LANES), f32),
        ),
        in_specs=[in_place],
        out_specs=(in_vmem,) * 4,
        scratch_shapes=[pltpu.VMEM((1, tiles), jnp.int32), one_copy],
        compiler_params=params,
        name="geometry",
    )(in_hbm(owners.reshape(1, tiles)))
    beside = tuple((name, lax.axis_size(name)) for name in everywhere)
    places = tiles + 2 * len(beside) * ghost_tiles
    for step_number in range(2):
        final = step_number == 1
        arrived = []
        for name, _ in beside:
            arrived.extend((even_pairs(ghosts, name), odd_pairs(ghosts, name)))
        if not final:
            strengths = arrived
        if final:
            slab = gather_moments(pack)
            slabs = (slab, even_pairs(slab, "gz")) if deep == 2 else (lax.psum(slab, "gz"),)
        else:
            received = lax.all_to_all(leaf, everywhere, split_axis=0, concat_axis=0, tiled=True)
        close = pl.pallas_call(
            functools.partial(near_kernel, tiles, ghost_tiles, deep, beside),
            out_shape=pack_type,
            in_specs=[in_place] * 2 + [in_vmem] * (1 + 2 * len(arrived)),
            out_specs=in_vmem,
            scratch_shapes=[
                pltpu.VMEM((places * FEATURES, LANES), bf16),
                pltpu.VMEM((tiles * FEATURES, LANES), bf16),
                pltpu.VMEM((places * 2 * ROWS, 2 * LANES), bf16),
                pltpu.VMEM((tiles * 2 * ROWS, LANES), f32),
                pltpu.SMEM(pair_targets.shape, jnp.int32),
                pltpu.SMEM(pair_sources.shape, jnp.int32),
                pltpu.SemaphoreType.DMA((2,)),
            ],
            compiler_params=params,
            name="near",
        )(in_hbm(pair_targets), in_hbm(pair_sources), pack, *arrived, *strengths)
        if not final:
            half_type = jax.ShapeDtypeStruct((ghost_tiles * 4, LANES), f32)
            pack, ghosts = pl.pallas_call(
                functools.partial(far_kernel, tiles, wide, tall, deep),
                out_shape=(pack_type, half_type),
                in_specs=[in_vmem] * 5,
                out_specs=(in_vmem,) * 2,
                scratch_shapes=[pltpu.VMEM((tiles * ROWS, LANES), f32), work, work, square],
                compiler_params=params,
                name="far",
            )(ghost_ids, pack, close, received, table)
    size = 6 * capacity + 4
    sent = pl.pallas_call(
        functools.partial(handover_kernel, tiles, group, capacity),
        out_shape=jax.ShapeDtypeStruct((group * size, LANES), f32),
        in_specs=[in_vmem] * (4 + len(slabs)),
        out_specs=in_vmem,
        compiler_params=params,
        name="handover",
    )(placer, flags, pack, close, *slabs)
    handed = lax.all_to_all(sent, ("gx", "gy"), split_axis=0, concat_axis=0, tiled=True)
    moved = jax.ShapeDtypeStruct((3, group * capacity, LANES), f32)
    moved = pl.pallas_call(
        functools.partial(finish_kernel, wide, tall, deep, capacity),
        out_shape=(moved, moved),
        in_specs=[in_vmem] * 2,
        out_specs=(in_vmem,) * 2,
        scratch_shapes=[
            work,
            pltpu.VMEM((group * group // LANES * TERMS * ROWS, LANES), f32),
            pltpu.VMEM((group * TERMS * ROWS, LANES), f32),
            square,
        ],
        compiler_params=params,
        name="finish",
    )(handed, pair_table)
    return tuple(value.transpose(1, 0, 2) for value in moved)


def solution(mesh):
    return jax.shard_map(
        per_device,
        mesh=mesh,
        in_specs=(
            P(None, everywhere),
            P(None, everywhere),
            P(everywhere),
            P(everywhere),
            P(everywhere),
            P(everywhere, None),
        ),
        out_specs=(P(everywhere, None, None), P(everywhere, None, None)),
        check_vma=False,
    )
```
